128 devices in a mesh: node: 64 (over z, y, x), freq: 2 (over core).
Axes of the slice: x: 4, y: 4, z: 4, core: 2. Of those that a mesh axis runs over, the one named last changes fastest.
Arguments:
- voltage: float32 [128, 1048576], P('freq', 'node'), may hold values from -0.75 to 0.75
- node_cond: float32 [1048576], P('node'), may hold values from 0.5 to 2
- model_table: float32 [6, 64], replicated, may hold values from 0.25 to 1.5
- model_index: int32 [262144], P('node'), may hold values from 0 to 63
- send_nodes: int32 [64, 64, 2, 128], P('node'), may hold values from 0 to 16384, as said below
- term_slot: int32 [4, 262144], P(None, 'node'), may hold values from 0 to 8191, as said below
Outputs:
- residual: float32 [128, 1048576], P('freq', 'node')
The draws below stay inside these ranges and needn't reach their ends.
Inputs may be any that keep to these rules, and one draw needn't show every extreme that they name: Each list send_nodes[s, d, g] names local node indices of node group s (0 to 16383) in its first entries and 16384, an empty slot, in the rest; every list has at least one node and the lists of a node group to itself are full. `term_slot`: entry s * 128 + j names row j of the list that node group s sends to the transistor's own node group and transistor group; that row is never empty.
All inputs are finite; a program needn't handle non-finite values.
Results may differ from the reference program's by a relative error of at most 0.000064.
Values sent between devices are 32-bit elements; how exact they have to be, the bound alone decides.
No kernel may reach another device: no remote copies, remote signals or barrier semaphores. Data moves between devices by JAX's collectives and lax.ppermute only.
A program may use at most 128 MiB of HBM per device.

```python
import jax
import jax.numpy as jnp
from jax import lax

NTIME = 128
NODE_DEV = 16384
TR_DEV = 4096
TR_LOCAL = 2048
SLOTS = 128
NMODEL = 64
NPARAM = 6
PEERS = 64
GROUPS = 2
NODES = 1048576
TRANSISTORS = 262144


def pair_counts(key):
    base_key = jax.random.fold_in(key, 17)
    top_count = min(SLOTS, max(1, 4 * TR_LOCAL // PEERS))
    low_count = max(1, 3 * top_count // 4)
    counts = jax.random.randint(base_key, (PEERS, PEERS, GROUPS), low_count, top_count + 1)
    on_diag = jnp.arange(PEERS)[:, None, None] == jnp.arange(PEERS)[None, :, None]
    return jnp.where(on_diag, SLOTS, counts).astype(jnp.int32)


def draw_send_nodes(key, part):
    counts = pair_counts(key)
    picked = jax.random.randint(jax.random.fold_in(key, 29), (PEERS, PEERS, GROUPS, SLOTS), 0, NODE_DEV)
    is_live = jnp.arange(SLOTS)[None, None, None, :] < counts[..., None]
    return jnp.where(is_live, picked, NODE_DEV).astype(jnp.int32)


def draw_term_slot(key, part):
    counts = pair_counts(key)
    group_total = TRANSISTORS // TR_LOCAL
    terminal_count = 4 * TR_LOCAL
    scores = jax.random.randint(jax.random.fold_in(key, 41), (group_total, terminal_count), 0, 16384)
    distinct = scores * terminal_count + jnp.arange(terminal_count, dtype=jnp.int32)[None, :]
    ranking = jnp.argsort(distinct, axis=1, stable=True).astype(jnp.int32)
    transistor = jnp.arange(TRANSISTORS, dtype=jnp.int32)
    owner_dev = (transistor // TR_DEV)[None, :]
    group_pos = (transistor % TR_DEV // TR_LOCAL)[None, :]
    group_id = (transistor // TR_LOCAL)[None, :]
    term_pos = jnp.arange(4, dtype=jnp.int32)[:, None] * TR_LOCAL + (transistor % TR_LOCAL)[None, :]
    rank_value = ranking[group_id, term_pos]
    source_dev = (owner_dev + rank_value % PEERS) % PEERS
    live_count = counts[source_dev, owner_dev, group_pos]
    row_pos = rank_value // PEERS % live_count
    return (source_dev * SLOTS + row_pos).astype(jnp.int32)


def place_ends(result, stream_key, smallest, largest):
    longest = result.shape.index(max(result.shape))
    spots = []
    for shift in (0, 1):
        where = [jax.random.randint(jax.random.fold_in(stream_key, axis), (), 0, length) for axis, length in enumerate(result.shape)]
        where[longest] = (where[longest] + shift) % result.shape[longest]
        spots.append(tuple(where))
    return result.at[spots[0]].set(smallest).at[spots[1]].set(largest)


def block_levels(key, extent, pieces, least, largest):
    gain, own = 1.0, jax.random.fold_in(key, 6)
    for position, blocks in pieces:
        heights = jnp.exp(jax.random.uniform(jax.random.fold_in(own, position), (blocks,), jnp.float32, least / len(pieces), largest / len(pieces)))
        gain = gain * jnp.repeat(heights, extent[position] // blocks).reshape([-1 if axis == position else 1 for axis in range(len(extent))])
    return gain


def centred(own_key, extent, scale, limit, pieces=(), kind=jnp.bfloat16):
    gain = block_levels(own_key, extent, pieces, -0.22, 0.18) if pieces else 1.0
    result = jax.random.normal(own_key, extent, jnp.float32) * scale * gain
    return jnp.minimum(jnp.maximum(result, -limit), limit).astype(kind)


def setup_inputs(seed: int = 0) -> dict:
    arg_keys = jax.random.split(jax.random.key(seed), 7)
    return {
        "voltage": centred(arg_keys[0], (NTIME, NODES), 0.125, 0.75, ((0, 2), (1, 64)), jnp.float32),
        "node_cond": jnp.clip(0.5 + 1.5 * jax.random.uniform(arg_keys[1], (NODES,), jnp.float32) ** block_levels(arg_keys[1], (NODES,), ((0, 64),), -0.2, 0.2), 0.5, 2.0),
        "model_table": jnp.clip(jax.random.uniform(arg_keys[2], (NPARAM, NMODEL), jnp.float32, 0.25, 1.5), 0.25, 1.5),
        "model_index": place_ends(jax.random.randint(arg_keys[3], (TRANSISTORS,), 0, NMODEL), jax.random.fold_in(arg_keys[3], 1), 0, NMODEL - 1).astype(jnp.int32),
        "send_nodes": draw_send_nodes(jax.random.fold_in(arg_keys[6], 71), 0),
        "term_slot": draw_term_slot(jax.random.fold_in(arg_keys[6], 71), 0),
    }


OMEGA = 0.05
HIGH = lax.Precision.HIGHEST


def dft_tables(npoints):
    half_len = npoints // 2
    time_idx = jnp.arange(npoints, dtype=jnp.int32)[:, None]
    row_idx = jnp.arange(npoints, dtype=jnp.int32)[None, :]
    is_sine = (row_idx >= half_len) & (row_idx < npoints - 1)
    edge_row = (row_idx == 0) | (row_idx == npoints - 1)
    harmonic = jnp.where(row_idx < half_len, row_idx, jnp.where(row_idx == npoints - 1, half_len, row_idx - half_len + 1))
    phases = (2.0 * jnp.pi / npoints) * ((time_idx * harmonic) % npoints).astype(jnp.float32)
    basis_rows = jnp.where(is_sine, jnp.sin(phases), jnp.cos(phases))
    weight = jnp.where(edge_row, 1.0 / npoints, 2.0 / npoints).astype(jnp.float32)
    deriv_rate = OMEGA * harmonic.astype(jnp.float32) * weight
    slope_rows = jnp.where(is_sine, -deriv_rate * jnp.cos(phases), jnp.where(edge_row, 0.0, deriv_rate * jnp.sin(phases)))
    return basis_rows, (weight * basis_rows).T, slope_rows.T


def soft_bend(values):
    return values + 0.5 * jnp.tanh(values)


def compact_model(term_volts, params):
    drain_v = term_volts[:, 0]
    gate_v = term_volts[:, 1]
    source_v = term_volts[:, 2]
    bulk_v = term_volts[:, 3]
    pinch_v = (gate_v - params[0]) / (1.0 + params[2])
    forward = jnp.square(jax.nn.softplus(0.5 * (pinch_v - source_v)))
    reverse = jnp.square(jax.nn.softplus(0.5 * (pinch_v - drain_v)))
    channel = params[1] * (forward - reverse)
    quiet = jnp.zeros_like(channel)
    current = jnp.stack([channel, quiet, -channel, quiet], axis=1)
    gate_src = params[3] * soft_bend(gate_v - source_v)
    gate_drn = params[4] * soft_bend(gate_v - drain_v)
    drain_blk = params[5] * soft_bend(drain_v - bulk_v)
    charge = jnp.stack([drain_blk - gate_drn, gate_src + gate_drn, -gate_src, -drain_blk], axis=1)
    return current, charge


def model_params(table, indices):
    onehot = (jnp.arange(table.shape[1], dtype=jnp.int32)[:, None] == indices[None, :]).astype(jnp.float32)
    return jnp.dot(table, onehot, precision=HIGH)


def reference(voltage, node_cond, model_table, model_index, send_nodes, term_slot):
    transistor = jnp.arange(TRANSISTORS, dtype=jnp.int32)
    owner_dev = (transistor // TR_DEV)[None, :]
    group_pos = ((transistor % TR_DEV) // TR_LOCAL)[None, :]
    source_dev = term_slot // SLOTS
    slot_pos = term_slot % SLOTS
    node_ids = source_dev * NODE_DEV + send_nodes[source_dev, owner_dev, group_pos, slot_pos]
    synthesis, analysis, slope_table = dft_tables(NTIME)
    term_volts = jnp.take(voltage, node_ids.reshape(-1), axis=1).reshape(NTIME, 4, TRANSISTORS)
    waveforms = jnp.einsum("th,hkn->tkn", synthesis, term_volts, precision=HIGH)
    params = model_params(model_table, model_index)
    current, charge = compact_model(waveforms, params)
    amplitudes = jnp.einsum("ht,tkn->hkn", analysis, current, precision=HIGH) + jnp.einsum("ht,tkn->hkn", slope_table, charge, precision=HIGH)
    residual = node_cond[None, :] * voltage
    return residual.at[:, node_ids.reshape(-1)].add(amplitudes.reshape(NTIME, -1))
```

```python
import jax
import jax.numpy as jnp
import numpy as np
from jax import lax
from jax.experimental import pallas as pl
from jax.experimental.pallas import tpu as pltpu
from jax.sharding import PartitionSpec as P

OMEGA = 0.05
HIGH = lax.Precision.HIGHEST
F32 = jnp.float32
BF16 = jnp.bfloat16


def dft_tables(npoints):
    half_len = npoints // 2
    time_idx = np.arange(npoints)[:, None]
    row_idx = np.arange(npoints)[None, :]
    is_sine = (row_idx >= half_len) & (row_idx < npoints - 1)
    edge_row = (row_idx == 0) | (row_idx == npoints - 1)
    harmonic = np.where(row_idx < half_len, row_idx, np.where(row_idx == npoints - 1, half_len, row_idx - half_len + 1))
    phases = 2.0 * np.pi / npoints * (time_idx * harmonic % npoints)
    basis_rows = np.where(is_sine, np.sin(phases), np.cos(phases))
    weight = np.where(edge_row, 1.0 / npoints, 2.0 / npoints)
    deriv_rate = OMEGA * harmonic * weight
    slope_rows = np.where(is_sine, -deriv_rate * np.cos(phases), np.where(edge_row, 0.0, deriv_rate * np.sin(phases)))
    return basis_rows, (weight * basis_rows).T, slope_rows.T


def split_weights(w):
    w = w.astype(np.float32)
    hi = w.astype(jnp.bfloat16)
    lo = (w - hi.astype(np.float32)).astype(jnp.bfloat16)
    return jnp.asarray(hi), jnp.asarray(lo)


def dot3(x, w_hi, w_lo):
    x_hi = x.astype(BF16)
    x_lo = (x - x_hi.astype(F32)).astype(BF16)
    out = jnp.dot(x_hi, w_hi, preferred_element_type=F32)
    out = out + jnp.dot(x_hi, w_lo, preferred_element_type=F32)
    return out + jnp.dot(x_lo, w_hi, preferred_element_type=F32)


def soft_bend(values):
    return values + 0.5 * jnp.tanh(values)


def softplus(x):
    return jnp.maximum(x, 0.0) + jnp.log1p(jnp.exp(-jnp.abs(x)))


def pick_kernel(rows, slots, idx, v_hbm, out_hbm, vbuf, table, obuf, in_sem, out_sem):
    nodes = vbuf.shape[1]
    n_in = in_sem.shape[0]
    n_out = out_sem.shape[0]
    width = nodes // n_in
    half = slots // 2
    peers = obuf.shape[0] // half
    per_out = peers // n_out

    def fetch(c):
        cols = pl.ds(c * width, width)
        return pltpu.make_async_copy(v_hbm.at[:, cols], vbuf.at[:, cols], in_sem.at[c])

    def ship(c):
        part = pl.ds(c * per_out * half, per_out * half)
        return pltpu.make_async_copy(obuf.at[part], out_hbm.at[part], out_sem.at[c])

    for c in range(n_in):
        fetch(c).start()
    table[pl.ds(nodes, 8), :] = jnp.zeros((8, 128), F32)
    for c in range(n_in):
        fetch(c).wait()

        def turn(b, carry, c=c):
            at = pl.multiple_of(c * width + b * 128, 128)
            x = vbuf[:, pl.ds(at, 128)]
            table[pl.ds(at, 128), :] = jnp.concatenate([x, x], axis=0).T
            return carry

        lax.fori_loop(0, width // 128, turn, 0)
    low = lax.broadcasted_iota(jnp.int32, (1, 128), 1) < rows

    def group(c, carry):
        def peer(q, carry):
            p = c * per_out + q
            for j in range(half):
                a = idx[p * slots + j]
                b = idx[p * slots + half + j]
                obuf[pl.ds(p * half + j, 1), :] = jnp.where(low, table[pl.ds(a, 1), :], table[pl.ds(b, 1), :])
            return carry

        lax.fori_loop(0, per_out, peer, 0)
        ship(c).start()
        return carry

    lax.fori_loop(0, n_out, group, 0)
    for c in range(n_out):
        ship(c).wait()


def device_kernel(
    idx, params, syn_hi, syn_lo, ana_hi, ana_lo, x_hbm, out_hbm,
    xbuf, wave, gbuf, qbuf, abuf, acc0, acc1, acc2, acc3, in_sem, out_sem,
):
    accs = (acc0, acc1, acc2, acc3)
    senders, _, half, lanes = xbuf.shape
    n_in = in_sem.shape[0]
    n_out = out_sem.shape[0]
    per_in = senders // n_in
    per_out = senders // n_out
    tr_local = params.shape[0]
    chunk = gbuf.shape[1]
    sub = 64

    def fetch(c):
        part = pl.ds(c * per_in, per_in)
        return pltpu.make_async_copy(x_hbm.at[part], xbuf.at[part], in_sem.at[c])

    def ship(c):
        part = pl.ds(c * per_out, per_out)
        return pltpu.make_async_copy(xbuf.at[part], out_hbm.at[part], out_sem.at[c])

    for c in range(n_in):
        fetch(c).start()

    def clear(i, carry):
        for acc in accs:
            acc[pl.ds(pl.multiple_of(i * 256, 256), 256), :] = jnp.zeros((256, lanes), F32)
        return carry

    lax.fori_loop(0, acc0.shape[0] // 256, clear, 0)

    def synth(c, carry):
        fetch(c).wait()
        x = xbuf[pl.ds(c * per_in, per_in)]
        xx = jnp.concatenate(
            [x[:, 0].reshape(per_in * half, lanes), x[:, 1].reshape(per_in * half, lanes)], axis=1
        )
        y = dot3(xx, syn_hi[...], syn_lo[...])
        for s in range(per_in):
            at = pl.multiple_of((c * per_in + s) * 2 * half, 2 * half)
            wave[pl.ds(at, half), :] = y[s * half : (s + 1) * half, :lanes]
            wave[pl.ds(at + half, half), :] = y[s * half : (s + 1) * half, lanes:]
        return carry

    lax.fori_loop(0, n_in, synth, 0)

    def block(c, carry):
        base = c * chunk

        def collect(i, carry):
            t = i * 16
            for u in range(16):
                for k in range(4):
                    gbuf[k, pl.ds(t + u, 1), :] = wave[pl.ds(idx[k * tr_local + base + t + u], 1), :]
            return carry

        lax.fori_loop(0, chunk // 16, collect, 0)

        def model(i, carry):
            at = pl.ds(pl.multiple_of(i * sub, sub), sub)
            par = params[pl.ds(pl.multiple_of(base + i * sub, sub), sub), :]
            thresh, strength, inv_slope, cap_gs, cap_gd, cap_db = (par[:, m : m + 1] for m in range(6))
            drain, gate, source, bulk = (gbuf[k, at, :] for k in range(4))
            pinch = (gate - thresh) * inv_slope
            forward = softplus(0.5 * (pinch - source))
            reverse = softplus(0.5 * (pinch - drain))
            qbuf[at, 0:lanes] = strength * (forward * forward - reverse * reverse)
            qbuf[at, lanes : 2 * lanes] = cap_gs * soft_bend(gate - source)
            qbuf[at, 2 * lanes : 3 * lanes] = cap_gd * soft_bend(gate - drain)
            qbuf[at, 3 * lanes : 4 * lanes] = cap_db * soft_bend(drain - bulk)
            return carry

        lax.fori_loop(0, chunk // sub, model, 0)
        left = dot3(qbuf[:, : 2 * lanes], ana_hi[:, : 2 * lanes], ana_lo[:, : 2 * lanes])
        right = dot3(qbuf[:, 2 * lanes :], ana_hi[:, 2 * lanes :], ana_lo[:, 2 * lanes :])
        chan, gs = left[:, :lanes], left[:, lanes:]
        gd, db = right[:, :lanes], right[:, lanes:]
        abuf[0] = chan + (db - gd)
        abuf[1] = gs + gd
        abuf[2] = -chan - gs
        abuf[3] = -db

        def spread(i, carry):
            t = i * 8
            for u in range(8):
                for k in range(4):
                    row = pl.ds(idx[k * tr_local + base + t + u], 1)
                    accs[k][row, :] = accs[k][row, :] + abuf[k, pl.ds(t + u, 1), :]
            return carry

        lax.fori_loop(0, chunk // 8, spread, 0)
        return carry

    lax.fori_loop(0, tr_local // chunk, block, 0)
    low = lax.broadcasted_iota(jnp.int32, (half, lanes), 1) < half

    def pack(c, carry):
        for s in range(per_out):
            peer = c * per_out + s
            at = pl.multiple_of(peer * 2 * half, 2 * half)
            first = sum(acc[pl.ds(at, half), :] for acc in accs)
            second = sum(acc[pl.ds(at + half, half), :] for acc in accs)
            xbuf[peer, 0] = jnp.where(low, first, pltpu.roll(second, half, 1))
            xbuf[peer, 1] = jnp.where(low, pltpu.roll(first, half, 1), second)
        ship(c).start()
        return carry

    lax.fori_loop(0, n_out, pack, 0)
    for c in range(n_out):
        ship(c).wait()


def residual_kernel(
    rows, slots, idx, cond, x_hbm, v_hbm, out_hbm,
    xbuf, vbuf, low0, low1, high0, high1, in_sem, v_sem, out_sem,
):
    nodes = vbuf.shape[1]
    half = slots // 2
    n_in = in_sem.shape[0]
    n_out = out_sem.shape[0]
    width = nodes // n_out
    peers = xbuf.shape[0] // half
    per_in = peers // n_in

    def fetch(c):
        part = pl.ds(c * per_in * half, per_in * half)
        return pltpu.make_async_copy(x_hbm.at[part], xbuf.at[part], in_sem.at[c])

    def ship(c):
        cols = pl.ds(c * width, width)
        return pltpu.make_async_copy(vbuf.at[:, cols], out_hbm.at[:, cols], out_sem.at[c])

    v_copy = pltpu.make_async_copy(v_hbm, vbuf, v_sem)
    for c in range(n_in):
        fetch(c).start()
    v_copy.start()

    def clear(i, carry):
        for acc in (low0, low1, high0, high1):
            acc[pl.ds(pl.multiple_of(i * 256, 256), 256), :] = jnp.zeros((256, 128), F32)
        return carry

    lax.fori_loop(0, nodes // 256, clear, 0)

    def group(c, carry):
        fetch(c).wait()

        def peer(q, carry):
            p = c * per_in + q
            for j in range(half):
                acc_a, acc_b = ((low0, high0), (low1, high1))[j % 2]
                x = xbuf[pl.ds(p * half + j, 1), :]
                a = pl.ds(idx[p * slots + j], 1)
                b = pl.ds(idx[p * slots + half + j], 1)
                acc_a[a, :] = acc_a[a, :] + x
                acc_b[b, :] = acc_b[b, :] + x
            return carry

        lax.fori_loop(0, per_in, peer, 0)
        return carry

    lax.fori_loop(0, n_in, group, 0)
    v_copy.wait()
    low = lax.broadcasted_iota(jnp.int32, (128, 128), 1) < rows

    def finish(c, carry):
        def turn(b, carry):
            at = pl.multiple_of(c * width + b * 128, 128)
            part = pl.ds(at, 128)
            both = jnp.where(low, low0[part, :] + low1[part, :], high0[part, :] + high1[part, :]).T
            cols = pl.ds(at, 128)
            vbuf[:, cols] = vbuf[:, cols] * cond[:, cols] + (both[:rows] + both[rows:])
            return carry

        lax.fori_loop(0, width // 128, turn, 0)
        ship(c).start()
        return carry

    lax.fori_loop(0, n_out, finish, 0)
    for c in range(n_out):
        ship(c).wait()


SMEM = pl.BlockSpec(memory_space=pltpu.SMEM)
VMEM = pl.BlockSpec(memory_space=pltpu.VMEM)
ANY = pl.BlockSpec(memory_space=pl.ANY)
ROOM = pltpu.CompilerParams(vmem_limit_bytes=60 * 2**20)


def per_device(voltage, node_cond, model_table, model_index, send_nodes, term_slot):
    rows, nodes = voltage.shape
    senders = send_nodes.shape[1]
    groups = send_nodes.shape[2]
    slots = send_nodes.shape[3]
    half = slots // 2
    peers = senders * groups
    lanes = rows * groups
    tr_local = term_slot.shape[1] // groups
    send_list = send_nodes.reshape(-1)

    outgoing = pl.pallas_call(
        lambda *refs: pick_kernel(rows, slots, *refs),
        out_shape=jax.ShapeDtypeStruct((peers * half, lanes), F32),
        in_specs=[SMEM, ANY],
        out_specs=ANY,
        scratch_shapes=[
            pltpu.VMEM((rows, nodes), F32),
            pltpu.VMEM((nodes + 8, lanes), F32),
            pltpu.VMEM((peers * half, lanes), F32),
            pltpu.SemaphoreType.DMA((8,)),
            pltpu.SemaphoreType.DMA((8,)),
        ],
        compiler_params=ROOM,
        name="pick",
    )(send_list, voltage)

    arrived = lax.all_to_all(outgoing.reshape(peers, half, lanes), ("node", "freq"), 0, 0, tiled=True)

    start = lax.axis_index("freq") * tr_local
    index = lax.dynamic_slice_in_dim(model_index, start, tr_local)
    slot_list = lax.dynamic_slice_in_dim(term_slot, start, tr_local, axis=1).reshape(-1)
    cards = jnp.concatenate([model_table[:2], 1.0 / (1.0 + model_table[2:3]), model_table[3:]], axis=0)
    onehot = (index[:, None] == jnp.arange(cards.shape[1], dtype=jnp.int32)[None, :]).astype(F32)
    params = jnp.dot(onehot, cards.T, precision=HIGH)

    synthesis, analysis, slope_table = dft_tables(lanes)
    syn = np.zeros((2, 2, rows, 2, lanes))
    for f in range(2):
        for q in range(2):
            syn[f, q, :, q, :] = synthesis.T[f * rows : (f + 1) * rows]
    none = np.zeros((lanes, lanes))
    ana = np.concatenate(
        [np.block([[analysis.T, none], [none, slope_table.T]]), np.block([[slope_table.T, none], [none, slope_table.T]])],
        axis=1,
    )
    syn_hi, syn_lo = split_weights(syn.reshape(2 * lanes, 2 * lanes))
    ana_hi, ana_lo = split_weights(ana)
    chunk = 256

    returned = pl.pallas_call(
        device_kernel,
        out_shape=jax.ShapeDtypeStruct((senders, 2, half, lanes), F32),
        in_specs=[SMEM, VMEM, VMEM, VMEM, VMEM, VMEM, ANY],
        out_specs=ANY,
        scratch_shapes=[
            pltpu.VMEM((senders, 2, half, lanes), F32),
            pltpu.VMEM((senders * slots, lanes), F32),
            pltpu.VMEM((4, chunk, lanes), F32),
            pltpu.VMEM((chunk, 4 * lanes), F32),
            pltpu.VMEM((4, chunk, lanes), F32),
        ]
        + [pltpu.VMEM((senders * slots, lanes), F32)] * 4
        + [pltpu.SemaphoreType.DMA((8,)), pltpu.SemaphoreType.DMA((8,))],
        compiler_params=ROOM,
        name="devices",
    )(slot_list, params, syn_hi, syn_lo, ana_hi, ana_lo, arrived.reshape(senders, 2, half, lanes))

    incoming = lax.all_to_all(returned.reshape(peers, half, lanes), ("node", "freq"), 0, 0, tiled=True)

    return pl.pallas_call(
        lambda *refs: residual_kernel(rows, slots, *refs),
        out_shape=jax.ShapeDtypeStruct((rows, nodes), F32),
        in_specs=[SMEM, VMEM, ANY, ANY],
        out_specs=ANY,
        scratch_shapes=[pltpu.VMEM((peers * half, lanes), F32), pltpu.VMEM((rows, nodes), F32)]
        + [pltpu.VMEM((nodes + 8, lanes), F32)] * 4
        + [pltpu.SemaphoreType.DMA((8,)), pltpu.SemaphoreType.DMA, pltpu.SemaphoreType.DMA((8,))],
        compiler_params=ROOM,
        name="residual",
    )(send_list, node_cond.reshape(1, nodes), incoming.reshape(peers * half, lanes), voltage)


def solution(mesh):
    return jax.shard_map(
        per_device,
        mesh=mesh,
        in_specs=(
            P("freq", "node"),
            P("node"),
            P(),
            P("node"),
            P("node", None, None, None),
            P(None, "node"),
        ),
        out_specs=P("freq", "node"),
        check_vma=False,
    )
```

```python
import jax
import jax.numpy as jnp
import numpy as np
from jax import lax
from jax.experimental import pallas as pl
from jax.experimental.pallas import tpu as pltpu
from jax.sharding import PartitionSpec as P

OMEGA = 0.05
HIGH = lax.Precision.HIGHEST
F32 = jnp.float32
BF16 = jnp.bfloat16
BATCH = 16
TEAM = 8


def dft_tables(npoints):
    half_len = npoints // 2
    time_idx = np.arange(npoints)[:, None]
    row_idx = np.arange(npoints)[None, :]
    is_sine = (row_idx >= half_len) & (row_idx < npoints - 1)
    edge_row = (row_idx == 0) | (row_idx == npoints - 1)
    harmonic = np.where(row_idx < half_len, row_idx, np.where(row_idx == npoints - 1, half_len, row_idx - half_len + 1))
    phases = 2.0 * np.pi / npoints * (time_idx * harmonic % npoints)
    basis_rows = np.where(is_sine, np.sin(phases), np.cos(phases))
    weight = np.where(edge_row, 1.0 / npoints, 2.0 / npoints)
    deriv_rate = OMEGA * harmonic * weight
    slope_rows = np.where(is_sine, -deriv_rate * np.cos(phases), np.where(edge_row, 0.0, deriv_rate * np.sin(phases)))
    return basis_rows, (weight * basis_rows).T, slope_rows.T


def split_weights(w):
    w = w.astype(np.float32)
    hi = w.astype(jnp.bfloat16)
    lo = (w - hi.astype(np.float32)).astype(jnp.bfloat16)
    return jnp.asarray(hi), jnp.asarray(lo)


def dot3(x, w_hi, w_lo):
    x_hi = x.astype(BF16)
    x_lo = (x - x_hi.astype(F32)).astype(BF16)
    out = jnp.dot(x_hi, w_hi, preferred_element_type=F32)
    out = out + jnp.dot(x_hi, w_lo, preferred_element_type=F32)
    return out + jnp.dot(x_lo, w_hi, preferred_element_type=F32)


def soft_bend(values):
    return values + 0.5 * jnp.tanh(values)


def softplus(x):
    return jnp.maximum(x, 0.0) + jnp.log1p(jnp.exp(-jnp.abs(x)))


def pick_kernel(rows, slots, idx_hbm, v_hbm, out_hbm, idx, vbuf, table, obuf, idx_sem, in_sem, out_sem):
    nodes = vbuf.shape[1]
    n_in = in_sem.shape[0]
    n_out = out_sem.shape[0]
    width = nodes // n_in
    half = slots // 2
    peers = obuf.shape[0] // half
    per_out = peers // n_out

    def fetch(c):
        cols = pl.ds(c * width, width)
        return pltpu.make_async_copy(v_hbm.at[:, cols], vbuf.at[:, cols], in_sem.at[c])

    def ship(c):
        part = pl.ds(c * per_out * half, per_out * half)
        return pltpu.make_async_copy(obuf.at[part], out_hbm.at[part], out_sem.at[c])

    for c in range(n_in):
        fetch(c).start()
    idx_copy = pltpu.make_async_copy(idx_hbm, idx, idx_sem)
    idx_copy.start()
    table[pl.ds(nodes, 8), :] = jnp.zeros((8, 128), F32)
    low = lax.broadcasted_iota(jnp.int32, (128, 128), 1) < rows
    for c in range(n_in):
        fetch(c).wait()

        def turn(b, carry, c=c):
            for w in range(2):
                at = pl.multiple_of(c * width + (b * 2 + w) * 256, 256)
                x = jnp.concatenate([vbuf[:, pl.ds(at, 128)], vbuf[:, pl.ds(at + 128, 128)]], axis=0).T
                y = pltpu.roll(x, rows, 1)
                table[pl.ds(at, 128), :] = jnp.where(low, x, y)
                table[pl.ds(at + 128, 128), :] = jnp.where(low, y, x)
            return carry

        lax.fori_loop(0, width // 512, turn, 0)
    idx_copy.wait()

    for c in range(n_out):

        def rounds(i, carry, c=c):
            for w in range(4):
                j = i * 4 + w
                for p in range(c * per_out, (c + 1) * per_out):
                    a = table[pl.ds(idx.at[pl.ds(p * slots, half)][j], 1), :]
                    b = table[pl.ds(idx.at[pl.ds(p * slots + half, half)][j], 1), :]
                    obuf.at[pl.ds(p * half, half)][pl.ds(j, 1), :] = jnp.where(low[:1], a, b)
            return carry

        lax.fori_loop(0, half // 4, rounds, 0)
        ship(c).start()
    for c in range(n_out):
        ship(c).wait()


def add_rows(table, names, rows):
    spots = [pl.ds(name, 1) for name in names]
    sums = [table[spot, :] + row for spot, row in zip(spots, rows)]
    for spot, total in zip(spots, sums):
        table[spot, :] = total


def device_kernel(
    idx_hbm, first_hbm, flags_hbm, params_hbm, syn_hi_hbm, syn_lo_hbm, ana_hi_hbm, ana_lo_hbm, x_hbm, out_hbm,
    idx, first, flags, params, syn_hi, syn_lo, ana_hi, ana_lo,
    xbuf, wave, gbuf, qbuf, abuf, acc0, acc1, acc2, acc3, own_sem, in_sem, out_sem,
):
    accs = (acc0, acc1, acc2, acc3)
    senders, _, half, lanes = xbuf.shape
    n_in = in_sem.shape[0]
    n_out = out_sem.shape[0]
    per_in = senders // n_in
    per_out = senders // n_out
    tr_local = params.shape[0]
    chunk = gbuf.shape[1]
    batches = tr_local // BATCH
    sub = 64

    def fetch(c):
        part = pl.ds(c * per_in, per_in)
        return pltpu.make_async_copy(x_hbm.at[part], xbuf.at[part], in_sem.at[c])

    def ship(c):
        part = pl.ds(c * per_out, per_out)
        return pltpu.make_async_copy(xbuf.at[part], out_hbm.at[part], out_sem.at[c])

    own = [
        pltpu.make_async_copy(source, copy, own_sem.at[i])
        for i, (source, copy) in enumerate(
            [
                (syn_hi_hbm, syn_hi), (syn_lo_hbm, syn_lo), (idx_hbm, idx), (params_hbm, params),
                (ana_hi_hbm, ana_hi), (ana_lo_hbm, ana_lo), (first_hbm, first), (flags_hbm, flags),
            ]
        )
    ]
    for copy in own[:2]:
        copy.start()
    for c in range(n_in):
        fetch(c).start()
    for copy in own[2:]:
        copy.start()

    def clear(i, carry):
        for acc in accs:
            acc[pl.ds(pl.multiple_of(i * 256, 256), 256), :] = jnp.zeros((256, lanes), F32)
        return carry

    lax.fori_loop(0, wave.shape[0] // 256, clear, 0)

    for copy in own[:2]:
        copy.wait()

    def synth(c, carry):
        fetch(c).wait()
        x = xbuf[pl.ds(c * per_in, per_in)]
        xx = jnp.concatenate(
            [x[:, 0].reshape(per_in * half, lanes), x[:, 1].reshape(per_in * half, lanes)], axis=1
        )
        y = dot3(xx, syn_hi[...], syn_lo[...])
        for s in range(per_in):
            at = pl.multiple_of((c * per_in + s) * 2 * half, 2 * half)
            wave[pl.ds(at, half), :] = y[s * half : (s + 1) * half, :lanes]
            wave[pl.ds(at + half, half), :] = y[s * half : (s + 1) * half, lanes:]
        return carry

    lax.fori_loop(0, n_in, synth, 0)
    for copy in own[2:]:
        copy.wait()

    def block(c, carry):
        base = c * chunk

        def collect(i, carry):
            b = c * (chunk // BATCH) + i
            t = pl.multiple_of(i * BATCH, BATCH)
            for k in range(4):
                block = gbuf.at[k, pl.ds(t, BATCH)]
                for u in range(BATCH):
                    block[u : u + 1, :] = wave[pl.ds(idx.at[pl.ds((k * BATCH + u) * batches, batches)][b], 1), :]
            return carry

        lax.fori_loop(0, chunk // BATCH, collect, 0)

        def model(i, carry):
            at = pl.ds(pl.multiple_of(i * sub, sub), sub)
            par = params[pl.ds(pl.multiple_of(base + i * sub, sub), sub), :]
            thresh, strength, inv_slope, cap_gs, cap_gd, cap_db = (par[:, m : m + 1] for m in range(6))
            drain, gate, source, bulk = (gbuf[k, at, :] for k in range(4))
            pinch = (gate - thresh) * inv_slope
            forward = softplus(0.5 * (pinch - source))
            reverse = softplus(0.5 * (pinch - drain))
            qbuf[at, 0:lanes] = strength * (forward * forward - reverse * reverse)
            qbuf[at, lanes : 2 * lanes] = cap_gs * soft_bend(gate - source)
            qbuf[at, 2 * lanes : 3 * lanes] = cap_gd * soft_bend(gate - drain)
            qbuf[at, 3 * lanes : 4 * lanes] = cap_db * soft_bend(drain - bulk)
            return carry

        lax.fori_loop(0, chunk // sub, model, 0)
        left = dot3(qbuf[:, : 2 * lanes], ana_hi[:, : 2 * lanes], ana_lo[:, : 2 * lanes])
        right = dot3(qbuf[:, 2 * lanes :], ana_hi[:, 2 * lanes :], ana_lo[:, 2 * lanes :])
        chan, gs = left[:, :lanes], left[:, lanes:]
        gd, db = right[:, :lanes], right[:, lanes:]
        abuf[0] = chan + (db - gd)
        abuf[1] = gs + gd
        abuf[2] = -chan - gs
        abuf[3] = -db

        def spread(i, carry):
            b = c * (chunk // BATCH) + i
            t = pl.multiple_of(i * BATCH, BATCH)
            for team in range(0, BATCH, TEAM):
                for k in range(4):
                    block = abuf.at[k, pl.ds(t, BATCH)]
                    add_rows(
                        accs[k],
                        [first.at[pl.ds((k * BATCH + u) * batches, batches)][b] for u in range(team, team + TEAM)],
                        [block[u : u + 1, :] for u in range(team, team + TEAM)],
                    )
            return carry

        lax.fori_loop(0, chunk // BATCH, spread, 0)

        def repeat(i, carry):
            b = c * (chunk // BATCH) + i

            @pl.when(flags[b] != 0)
            def _():
                for u in range(BATCH):
                    for k in range(4):
                        at = (k * BATCH + u) * batches + b
                        spot = pl.ds(jnp.where(first[at] == wave.shape[0], idx[at], wave.shape[0]), 1)
                        accs[k][spot, :] = accs[k][spot, :] + abuf[k, pl.ds(i * BATCH + u, 1), :]

            return carry

        lax.fori_loop(0, chunk // BATCH, repeat, 0)
        return carry

    lax.fori_loop(0, tr_local // chunk, block, 0)
    low = lax.broadcasted_iota(jnp.int32, (half, lanes), 1) < half

    def pack(c, carry):
        for s in range(per_out):
            peer = c * per_out + s
            at = pl.multiple_of(peer * 2 * half, 2 * half)
            first = sum(acc[pl.ds(at, half), :] for acc in accs)
            second = sum(acc[pl.ds(at + half, half), :] for acc in accs)
            xbuf[peer, 0] = jnp.where(low, first, pltpu.roll(second, half, 1))
            xbuf[peer, 1] = jnp.where(low, pltpu.roll(first, half, 1), second)
        ship(c).start()
        return carry

    lax.fori_loop(0, n_out, pack, 0)
    for c in range(n_out):
        ship(c).wait()


def residual_kernel(
    rows, slots, idx_hbm, first_hbm, flags_hbm, cond, x_hbm, v_hbm, out_hbm,
    idx, first, flags, xbuf, vbuf, low0, low1, high0, high1, own_sem, in_sem, v_sem, out_sem,
):
    nodes = vbuf.shape[1]
    half = slots // 2
    n_in = in_sem.shape[0]
    n_out = out_sem.shape[0]
    width = nodes // n_out
    peers = xbuf.shape[0] // half
    per_in = peers // n_in

    def fetch(c):
        part = pl.ds(c * per_in * half, per_in * half)
        return pltpu.make_async_copy(x_hbm.at[part], xbuf.at[part], in_sem.at[c])

    def ship(c):
        cols = pl.ds(c * width, width)
        return pltpu.make_async_copy(vbuf.at[:, cols], out_hbm.at[:, cols], out_sem.at[c])

    v_copy = pltpu.make_async_copy(v_hbm, vbuf, v_sem)
    own = [
        pltpu.make_async_copy(source, copy, own_sem.at[i])
        for i, (source, copy) in enumerate([(first_hbm, first), (flags_hbm, flags), (idx_hbm, idx)])
    ]
    fetch(0).start()
    for copy in own:
        copy.start()
    for c in range(1, n_in):
        fetch(c).start()
    v_copy.start()

    def clear(i, carry):
        for acc in (low0, low1, high0, high1):
            acc[pl.ds(pl.multiple_of(i * 256, 256), 256), :] = jnp.zeros((256, 128), F32)
        return carry

    lax.fori_loop(0, nodes // 256, clear, 0)

    tables = ((low0, high0), (low1, high1))
    for copy in own:
        copy.wait()

    for c in range(n_in):
        fetch(c).wait()
        mine = range(c * per_in, (c + 1) * per_in)

        def slot_pair(i, carry, mine=mine):
            for team in range(0, BATCH, TEAM):
                for w in range(2):
                    for h in range(2):
                        team_of = mine[team : team + TEAM]
                        add_rows(
                            tables[w][h],
                            [first.at[pl.ds(p * slots + h * half, half)][i * 2 + w] for p in team_of],
                            [xbuf.at[pl.ds(p * half, half)][pl.ds(i * 2 + w, 1), :] for p in team_of],
                        )
            return carry

        lax.fori_loop(0, half // 2, slot_pair, 0)

        def repeat(i, carry, c=c, mine=mine):
            @pl.when(flags[c * (half // 2) + i] != 0)
            def _():
                for w in range(2):

                    def one(q, carry):
                        p = c * per_in + q
                        x = xbuf[pl.ds(p * half + i * 2 + w, 1), :]
                        for h in range(2):
                            at = p * slots + h * half + i * 2 + w
                            spot = pl.ds(jnp.where(first[at] == nodes, idx[at], nodes), 1)
                            tables[w][h][spot, :] = tables[w][h][spot, :] + x
                        return carry

                    lax.fori_loop(0, BATCH, one, 0)

            return carry

        lax.fori_loop(0, half // 2, repeat, 0)
    v_copy.wait()
    low = lax.broadcasted_iota(jnp.int32, (128, 128), 1) < rows

    def finish(c, carry):
        def turn(b, carry):
            for w in range(2):
                at = pl.multiple_of(c * width + (b * 2 + w) * 256, 256)
                one, two = pl.ds(at, 128), pl.ds(at + 128, 128)
                one_low, one_high = low0[one, :] + low1[one, :], high0[one, :] + high1[one, :]
                two_low, two_high = low0[two, :] + low1[two, :], high0[two, :] + high1[two, :]
                both = jnp.where(low, one_low, two_high) + pltpu.roll(jnp.where(low, two_low, one_high), rows, 1)
                both = both.T
                vbuf[:, one] = vbuf[:, one] * cond[:, one] + both[:rows]
                vbuf[:, two] = vbuf[:, two] * cond[:, two] + both[rows:]
            return carry

        lax.fori_loop(0, width // 512, turn, 0)
        ship(c).start()
        return carry

    lax.fori_loop(0, n_out, finish, 0)
    for c in range(n_out):
        ship(c).wait()


def split_repeats(names, axis, spare):
    columns = [lax.index_in_dim(names, i, axis, keepdims=False) for i in range(names.shape[axis])]
    seen = [jnp.zeros(columns[0].shape, jnp.bool_)]
    for i in range(1, len(columns)):
        hit = columns[i] == columns[0]
        for j in range(1, i):
            hit = hit | (columns[i] == columns[j])
        seen.append(hit)
    seen = jnp.stack(seen, axis) & (names != spare)
    return jnp.where(seen, spare, names), seen


VMEM = pl.BlockSpec(memory_space=pltpu.VMEM)
ANY = pl.BlockSpec(memory_space=pl.ANY)
ROOM = pltpu.CompilerParams(vmem_limit_bytes=60 * 2**20)


def per_device(voltage, node_cond, model_table, model_index, send_nodes, term_slot):
    rows, nodes = voltage.shape
    senders = send_nodes.shape[1]
    groups = send_nodes.shape[2]
    slots = send_nodes.shape[3]
    half = slots // 2
    peers = senders * groups
    lanes = rows * groups
    tr_local = term_slot.shape[1] // groups
    send_list = send_nodes.reshape(-1)

    outgoing = pl.pallas_call(
        lambda *refs: pick_kernel(rows, slots, *refs),
        out_shape=jax.ShapeDtypeStruct((peers * half, lanes), F32),
        in_specs=[ANY, ANY],
        out_specs=ANY,
        scratch_shapes=[
            pltpu.SMEM((peers * slots,), jnp.int32),
            pltpu.VMEM((rows, nodes), F32),
            pltpu.VMEM((nodes + 8, lanes), F32),
            pltpu.VMEM((peers * half, lanes), F32),
            pltpu.SemaphoreType.DMA,
            pltpu.SemaphoreType.DMA((8,)),
            pltpu.SemaphoreType.DMA((8,)),
        ],
        compiler_params=ROOM,
        name="pick",
    )(send_list, voltage)

    arrived = lax.all_to_all(outgoing.reshape(peers, half, lanes), ("node", "freq"), 0, 0, tiled=True)

    start = lax.axis_index("freq") * tr_local
    index = lax.dynamic_slice_in_dim(model_index, start, tr_local)
    slot_grid = lax.dynamic_slice_in_dim(term_slot, start, tr_local, axis=1)
    batches = tr_local // BATCH
    index = index.reshape(BATCH, batches).T.reshape(-1)
    slot_list = slot_grid.reshape(-1)
    slot_grid = slot_grid.reshape(4 * BATCH // TEAM, TEAM, batches)
    tr_first, tr_seen = split_repeats(slot_grid, 1, senders * slots)
    tr_first = tr_first.reshape(-1)
    tr_flags = jnp.any(tr_seen, axis=(0, 1)).astype(jnp.int32)
    send_grid = send_list.reshape(peers // TEAM, TEAM, slots)
    send_first, send_seen = split_repeats(send_grid, 1, nodes)
    send_first = send_first.reshape(-1)
    send_flags = jnp.any(send_seen.reshape(peers // BATCH, BATCH, 2, half // 2, 2), axis=(1, 2, 4))
    send_flags = send_flags.astype(jnp.int32).reshape(-1)
    cards = jnp.concatenate([model_table[:2], 1.0 / (1.0 + model_table[2:3]), model_table[3:]], axis=0)
    onehot = (index[:, None] == jnp.arange(cards.shape[1], dtype=jnp.int32)[None, :]).astype(F32)
    params = jnp.dot(onehot, cards.T, precision=HIGH)

    synthesis, analysis, slope_table = dft_tables(lanes)
    syn = np.zeros((2, 2, rows, 2, lanes))
    for f in range(2):
        for q in range(2):
            syn[f, q, :, q, :] = synthesis.T[f * rows : (f + 1) * rows]
    none = np.zeros((lanes, lanes))
    ana = np.concatenate(
        [np.block([[analysis.T, none], [none, slope_table.T]]), np.block([[slope_table.T, none], [none, slope_table.T]])],
        axis=1,
    )
    syn_hi, syn_lo = split_weights(syn.reshape(2 * lanes, 2 * lanes))
    ana_hi, ana_lo = split_weights(ana)
    chunk = 256

    returned = pl.pallas_call(
        device_kernel,
        out_shape=jax.ShapeDtypeStruct((senders, 2, half, lanes), F32),
        in_specs=[ANY] * 9,
        out_specs=ANY,
        scratch_shapes=[pltpu.SMEM(a.shape, a.dtype) for a in (slot_list, tr_first, tr_flags)]
        + [pltpu.VMEM(a.shape, a.dtype) for a in (params, syn_hi, syn_lo, ana_hi, ana_lo)]
        + [
            pltpu.VMEM((senders, 2, half, lanes), F32),
            pltpu.VMEM((senders * slots, lanes), F32),
            pltpu.VMEM((4, chunk, lanes), F32),
            pltpu.VMEM((chunk, 4 * lanes), F32),
            pltpu.VMEM((4, chunk, lanes), F32),
        ]
        + [pltpu.VMEM((senders * slots + 8, lanes), F32)] * 4
        + [pltpu.SemaphoreType.DMA((8,))] * 3,
        compiler_params=ROOM,
        name="devices",
    )(slot_list, tr_first, tr_flags, params, syn_hi, syn_lo, ana_hi, ana_lo, arrived.reshape(senders, 2, half, lanes))

    incoming = lax.all_to_all(returned.reshape(peers, half, lanes), ("node", "freq"), 0, 0, tiled=True)

    return pl.pallas_call(
        lambda *refs: residual_kernel(rows, slots, *refs),
        out_shape=jax.ShapeDtypeStruct((rows, nodes), F32),
        in_specs=[ANY, ANY, ANY, VMEM, ANY, ANY],
        out_specs=ANY,
        scratch_shapes=[pltpu.SMEM(a.shape, a.dtype) for a in (send_list, send_first, send_flags)]
        + [pltpu.VMEM((peers * half, lanes), F32), pltpu.VMEM((rows, nodes), F32)]
        + [pltpu.VMEM((nodes + 8, lanes), F32)] * 4
        + [
            pltpu.SemaphoreType.DMA((3,)),
            pltpu.SemaphoreType.DMA((8,)),
            pltpu.SemaphoreType.DMA,
            pltpu.SemaphoreType.DMA((8,)),
        ],
        compiler_params=ROOM,
        name="residual",
    )(send_list, send_first, send_flags, node_cond.reshape(1, nodes), incoming.reshape(peers * half, lanes), voltage)


def solution(mesh):
    return jax.shard_map(
        per_device,
        mesh=mesh,
        in_specs=(
            P("freq", "node"),
            P("node"),
            P(),
            P("node"),
            P("node", None, None, None),
            P(None, "node"),
        ),
        out_specs=P("freq", "node"),
        check_vma=False,
    )
```

```python
import jax
import jax.numpy as jnp
import numpy as np
from jax import lax
from jax.experimental import pallas as pl
from jax.experimental.pallas import tpu as pltpu
from jax.sharding import PartitionSpec as P

OMEGA = 0.05
HIGH = lax.Precision.HIGHEST
F32 = jnp.float32
BF16 = jnp.bfloat16
BATCH = 16
TEAM = 4
STEP = 128


def dft_tables(npoints):
    half_len = npoints // 2
    time_idx = np.arange(npoints)[:, None]
    row_idx = np.arange(npoints)[None, :]
    is_sine = (row_idx >= half_len) & (row_idx < npoints - 1)
    edge_row = (row_idx == 0) | (row_idx == npoints - 1)
    harmonic = np.where(row_idx < half_len, row_idx, np.where(row_idx == npoints - 1, half_len, row_idx - half_len + 1))
    phases = 2.0 * np.pi / npoints * (time_idx * harmonic % npoints)
    basis_rows = np.where(is_sine, np.sin(phases), np.cos(phases))
    weight = np.where(edge_row, 1.0 / npoints, 2.0 / npoints)
    deriv_rate = OMEGA * harmonic * weight
    slope_rows = np.where(is_sine, -deriv_rate * np.cos(phases), np.where(edge_row, 0.0, deriv_rate * np.sin(phases)))
    return basis_rows, (weight * basis_rows).T, slope_rows.T


def split_weights(w):
    w = w.astype(np.float32)
    hi = w.astype(jnp.bfloat16)
    lo = (w - hi.astype(np.float32)).astype(jnp.bfloat16)
    return jnp.asarray(np.concatenate([hi, lo, hi], axis=0))


def dot3(x, w3):
    hi = x.astype(BF16)
    lo = (x - hi.astype(F32)).astype(BF16)
    return jnp.dot(jnp.concatenate([hi, hi, lo], axis=1), w3, preferred_element_type=F32)


def soft_bend(values):
    return values + 0.5 * jnp.tanh(values)


def softplus(x):
    return jnp.maximum(x, 0.0) + jnp.log1p(jnp.exp(-jnp.abs(x)))


def pick_kernel(rows, slots, idx_hbm, v_hbm, out_hbm, idx, vbuf, table, obuf, idx_sem, in_sem, out_sem):
    nodes = vbuf.shape[1]
    n_in = in_sem.shape[0]
    n_out = out_sem.shape[0]
    width = nodes // n_in
    half = slots // 2
    peers = obuf.shape[0] // half
    per_out = peers // n_out

    def fetch(c):
        cols = pl.ds(c * width, width)
        return pltpu.make_async_copy(v_hbm.at[:, cols], vbuf.at[:, cols], in_sem.at[c])

    def ship(c):
        part = pl.ds(c * per_out * half, per_out * half)
        return pltpu.make_async_copy(obuf.at[part], out_hbm.at[part], out_sem.at[c])

    for c in range(n_in):
        fetch(c).start()
    idx_copy = pltpu.make_async_copy(idx_hbm, idx, idx_sem)
    idx_copy.start()
    table[pl.ds(nodes, 8), :] = jnp.zeros((8, 128), F32)
    low = lax.broadcasted_iota(jnp.int32, (128, 128), 1) < rows
    for c in range(n_in):
        fetch(c).wait()

        def turn(b, carry, c=c):
            for w in range(8):
                at = pl.multiple_of(c * width + (b * 8 + w) * 256, 256)
                x = jnp.concatenate([vbuf[:, pl.ds(at, 128)], vbuf[:, pl.ds(at + 128, 128)]], axis=0).T
                y = pltpu.roll(x, rows, 1)
                table[pl.ds(at, 128), :] = jnp.where(low, x, y)
                table[pl.ds(at + 128, 128), :] = jnp.where(low, y, x)
            return carry

        lax.fori_loop(0, width // 2048, turn, 0)
    idx_copy.wait()

    for c in range(n_out):

        def rounds(i, carry, c=c):
            for w in range(8):
                j = i * 8 + w
                for p in range(c * per_out, (c + 1) * per_out):
                    a = table[pl.ds(idx.at[pl.ds(p * slots, half)][j], 1), :]
                    b = table[pl.ds(idx.at[pl.ds(p * slots + half, half)][j], 1), :]
                    obuf.at[pl.ds(p * half, half)][pl.ds(j, 1), :] = jnp.where(low[:1], a, b)
            return carry

        lax.fori_loop(0, half // 8, rounds, 0)
        ship(c).start()
    for c in range(n_out):
        ship(c).wait()


def add_rows(table, names, rows):
    spots = [pl.ds(name, 1) for name in names]
    sums = [table[spot, :] + row for spot, row in zip(spots, rows)]
    for spot, total in zip(spots, sums):
        table[spot, :] = total


def device_kernel(
    idx_hbm, first_hbm, flags_hbm, params_hbm, syn_hbm, ana_hbm, x_hbm, out_hbm,
    idx, first, flags, params, syn, ana,
    xbuf, wave, volts0, volts1, duo0, duo1, amps0, amps1, acc0, acc1, acc2, acc3, own_sem, in_sem, out_sem,
):
    accs = (acc0, acc1, acc2, acc3)
    volts, duos, amps = (volts0, volts1), (duo0, duo1), (amps0, amps1)
    senders, _, half, lanes = xbuf.shape
    n_in = in_sem.shape[0]
    n_out = out_sem.shape[0]
    per_in = senders // n_in
    per_out = senders // n_out
    tr_local = params.shape[0]
    batches = tr_local // BATCH
    step = volts0.shape[1]
    inner = step // BATCH
    steps = tr_local // step
    spare = wave.shape[0]

    def fetch(c):
        part = pl.ds(c * per_in, per_in)
        return pltpu.make_async_copy(x_hbm.at[part], xbuf.at[part], in_sem.at[c])

    def ship(c):
        part = pl.ds(c * per_out, per_out)
        return pltpu.make_async_copy(xbuf.at[part], out_hbm.at[part], out_sem.at[c])

    own = [
        pltpu.make_async_copy(source, copy, own_sem.at[i])
        for i, (source, copy) in enumerate(
            [
                (syn_hbm, syn), (idx_hbm, idx), (params_hbm, params),
                (ana_hbm, ana), (first_hbm, first), (flags_hbm, flags),
            ]
        )
    ]
    for copy in own[:1]:
        copy.start()
    for c in range(n_in):
        fetch(c).start()
    for copy in own[1:]:
        copy.start()
    for copy in own[:1]:
        copy.wait()
    rows_in = per_in * 2 * half

    def synth(c, carry):
        at = pl.multiple_of(c * rows_in, rows_in)
        for acc in accs:
            acc[pl.ds(at, rows_in), :] = jnp.zeros((rows_in, lanes), F32)
        fetch(c).wait()
        x = xbuf[pl.ds(c * per_in, per_in)]
        xx = jnp.concatenate(
            [x[:, 0].reshape(per_in * half, lanes), x[:, 1].reshape(per_in * half, lanes)], axis=1
        )
        y = dot3(xx, syn[...])
        for s in range(per_in):
            wave[pl.ds(at + s * 2 * half, half), :] = y[s * half : (s + 1) * half, :lanes]
            wave[pl.ds(at + (s * 2 + 1) * half, half), :] = y[s * half : (s + 1) * half, lanes:]
        return carry

    lax.fori_loop(0, n_in, synth, 0)
    for copy in own[1:]:
        copy.wait()

    def names_of(source, k, b):
        return [source.at[pl.ds((k * BATCH + u) * batches, batches)][b] for u in range(BATCH)]

    def collect(buf, i, q):
        for k in range(4):
            for u, name in enumerate(names_of(idx, k, i * inner + q)):
                buf[k, q * BATCH + u : q * BATCH + u + 1, :] = wave[pl.ds(name, 1), :]

    def model(buf, duo, i, q):
        at = pl.ds(q * BATCH, BATCH)
        par = params[pl.ds(pl.multiple_of(i * step + q * BATCH, BATCH), BATCH), :]
        thresh, strength, inv_slope, cap_gs, cap_gd, cap_db = (par[:, m : m + 1] for m in range(6))
        drain, gate, source, bulk = (buf[k, at, :] for k in range(4))
        pinch = (gate - thresh) * inv_slope
        forward = softplus(0.5 * (pinch - source))
        reverse = softplus(0.5 * (pinch - drain))
        duo[at, 0:lanes] = strength * (forward * forward - reverse * reverse)
        duo[at, lanes : 2 * lanes] = cap_gs * soft_bend(gate - source)
        duo[at, 2 * lanes : 3 * lanes] = cap_gd * soft_bend(gate - drain)
        duo[at, 3 * lanes : 4 * lanes] = cap_db * soft_bend(drain - bulk)

    def analyse(duo, amp):
        left = dot3(duo[:, : 2 * lanes], ana[:, : 2 * lanes])
        right = dot3(duo[:, 2 * lanes :], ana[:, 2 * lanes :])
        chan, gs = left[:, :lanes], left[:, lanes:]
        gd, db = right[:, :lanes], right[:, lanes:]
        amp[0] = chan + (db - gd)
        amp[1] = gs + gd
        amp[2] = -chan - gs
        amp[3] = -db

    def spread(amp, i, q):
        names = [names_of(first, k, i * inner + q) for k in range(4)]
        for team in range(0, BATCH, TEAM):
            for k in range(4):
                at = q * BATCH + team
                add_rows(
                    accs[k],
                    names[k][team : team + TEAM],
                    [amp[k, at + u : at + u + 1, :] for u in range(TEAM)],
                )

    def repeat(amp, i):
        @pl.when(flags[batches + i] != 0)
        def _():
            def batch(q, carry):
                b = i * inner + q

                @pl.when(flags[b] != 0)
                def _():
                    for u in range(BATCH):
                        for k in range(4):
                            at = (k * BATCH + u) * batches + b
                            spot = pl.ds(jnp.where(first[at] == spare, idx[at], spare), 1)
                            accs[k][spot, :] = accs[k][spot, :] + amp[k, pl.ds(q * BATCH + u, 1), :]

                return carry

            lax.fori_loop(0, inner, batch, 0)

    def stage(i, w, *, ahead=None, now=True, before=True, late=None):
        if before:
            analyse(duos[1 - w], amps[1 - w])
        for q in range(inner):
            if ahead is not None:
                collect(volts[1 - w], ahead, q)
            if now:
                model(volts[w], duos[w], i, q)
            if late is not None:
                spread(amps[w], late, q)
        if late is not None:
            repeat(amps[w], late)

    for q in range(inner):
        collect(volts0, 0, q)
    stage(0, 0, ahead=1, before=False)
    stage(1, 1, ahead=2)

    def pair(j, carry):
        for w in range(2):
            i = 2 * j + w
            stage(i, w, ahead=jnp.minimum(i + 1, steps - 1), late=i - 2)
        return carry

    lax.fori_loop(1, steps // 2, pair, 0)
    stage(steps, 0, now=False, late=steps - 2)
    stage(steps + 1, 1, now=False, before=False, late=steps - 1)
    low = lax.broadcasted_iota(jnp.int32, (half, lanes), 1) < half

    def pack(c, carry):
        for s in range(per_out):
            peer = c * per_out + s
            at = pl.multiple_of(peer * 2 * half, 2 * half)
            upper = pl.ds(at + half, half)
            at = pl.ds(at, half)
            one = sum(acc[at, :] for acc in accs)
            two = sum(acc[upper, :] for acc in accs)
            xbuf[peer, 0] = jnp.where(low, one, pltpu.roll(two, half, 1))
            xbuf[peer, 1] = jnp.where(low, pltpu.roll(one, half, 1), two)
        ship(c).start()
        return carry

    lax.fori_loop(0, n_out, pack, 0)
    for c in range(n_out):
        ship(c).wait()


def residual_kernel(
    rows, slots, idx_hbm, first_hbm, flags_hbm, cond_hbm, x_hbm, v_hbm, out_hbm,
    idx, first, flags, cond, xbuf, vbuf, low0, high0, low1, high1, own_sem, in_sem, v_sem, out_sem,
):
    nodes = vbuf.shape[1]
    half = slots // 2
    n_in = in_sem.shape[0]
    n_out = out_sem.shape[0]
    width = nodes // n_out
    peers = xbuf.shape[0] // half
    per_in = peers // n_in

    def fetch(c):
        part = pl.ds(c * per_in * half, per_in * half)
        return pltpu.make_async_copy(x_hbm.at[part], xbuf.at[part], in_sem.at[c])

    def ship(c):
        cols = pl.ds(c * width, width)
        return pltpu.make_async_copy(vbuf.at[:, cols], out_hbm.at[:, cols], out_sem.at[c])

    v_copy = pltpu.make_async_copy(v_hbm, vbuf, v_sem)
    own = [
        pltpu.make_async_copy(source, copy, own_sem.at[i])
        for i, (source, copy) in enumerate([(first_hbm, first), (flags_hbm, flags), (idx_hbm, idx), (cond_hbm, cond)])
    ]
    own[0].start()
    fetch(0).start()
    for copy in own[1:]:
        copy.start()
    for c in range(1, n_in):
        fetch(c).start()
    v_copy.start()

    def clear(i, carry):
        for acc in (low0, high0, low1, high1):
            acc[pl.ds(pl.multiple_of(i * 256, 256), 256), :] = jnp.zeros((256, 128), F32)
        return carry

    lax.fori_loop(0, nodes // 256, clear, 0)

    tables = ((low0, high0), (low1, high1))
    for copy in own:
        copy.wait()

    for c in range(n_in):
        fetch(c).wait()
        mine = range(c * per_in, (c + 1) * per_in)

        def slot_group(i, carry, mine=mine):
            for w in range(8):
                for team in range(0, BATCH, TEAM):
                    for h in range(2):
                        team_of = mine[team : team + TEAM]
                        add_rows(
                            tables[(team // TEAM) % 2][h],
                            [first.at[pl.ds(p * slots + h * half, half)][i * 8 + w] for p in team_of],
                            [xbuf.at[pl.ds(p * half, half)][pl.ds(i * 8 + w, 1), :] for p in team_of],
                        )
            return carry

        lax.fori_loop(0, half // 8, slot_group, 0)

        def repeat(i, carry, c=c, mine=mine):
            @pl.when(flags[c * half + i] != 0)
            def _():
                for q in range(BATCH):
                    x = xbuf[pl.ds(mine[q] * half + i, 1), :]
                    for h in range(2):
                        at = mine[q] * slots + h * half + i
                        spot = pl.ds(jnp.where(first[at] == nodes, idx[at], nodes), 1)
                        tables[0][h][spot, :] = tables[0][h][spot, :] + x

            return carry

        @pl.when(flags[n_in * (half + 8) + c] != 0)
        def _(repeat=repeat, c=c):
            def eighth(e, carry):
                @pl.when(flags[n_in * half + c * 8 + e] != 0)
                def _():
                    lax.fori_loop(0, half // 8, lambda i, z: repeat(e * (half // 8) + i, z), 0)

                return carry

            lax.fori_loop(0, 8, eighth, 0)

    v_copy.wait()
    low = lax.broadcasted_iota(jnp.int32, (128, 128), 1) < rows

    def finish(c, carry):
        def turn(b, carry):
            for w in range(8):
                at = pl.multiple_of(c * width + (b * 8 + w) * 256, 256)
                one, two = pl.ds(at, 128), pl.ds(at + 128, 128)
                both = jnp.where(low, low0[one, :] + low1[one, :], high0[two, :] + high1[two, :])
                both = both + pltpu.roll(jnp.where(low, low0[two, :] + low1[two, :], high0[one, :] + high1[one, :]), rows, 1)
                both = both.T
                vbuf[:, one] = vbuf[:, one] * cond[:, one] + both[:rows]
                vbuf[:, two] = vbuf[:, two] * cond[:, two] + both[rows:]
            return carry

        lax.fori_loop(0, width // 2048, turn, 0)
        ship(c).start()
        return carry

    lax.fori_loop(0, n_out, finish, 0)
    for c in range(n_out):
        ship(c).wait()


def split_repeats(names, axis, spare):
    columns = [lax.index_in_dim(names, i, axis, keepdims=False) for i in range(names.shape[axis])]
    seen = [jnp.zeros(columns[0].shape, jnp.bool_)]
    for i in range(1, len(columns)):
        hit = columns[i] == columns[0]
        for j in range(1, i):
            hit = hit | (columns[i] == columns[j])
        seen.append(hit)
    seen = jnp.stack(seen, axis) & (names != spare)
    return jnp.where(seen, spare, names), seen


ANY = pl.BlockSpec(memory_space=pl.ANY)
ROOM = pltpu.CompilerParams(vmem_limit_bytes=60 * 2**20)


def per_device(voltage, node_cond, model_table, model_index, send_nodes, term_slot):
    rows, nodes = voltage.shape
    senders = send_nodes.shape[1]
    groups = send_nodes.shape[2]
    slots = send_nodes.shape[3]
    half = slots // 2
    peers = senders * groups
    lanes = rows * groups
    tr_local = term_slot.shape[1] // groups
    send_list = send_nodes.reshape(-1)

    outgoing = pl.pallas_call(
        lambda *refs: pick_kernel(rows, slots, *refs),
        out_shape=jax.ShapeDtypeStruct((peers * half, lanes), F32),
        in_specs=[ANY, ANY],
        out_specs=ANY,
        scratch_shapes=[
            pltpu.SMEM((peers * slots,), jnp.int32),
            pltpu.VMEM((rows, nodes), F32),
            pltpu.VMEM((nodes + 8, lanes), F32),
            pltpu.VMEM((peers * half, lanes), F32),
            pltpu.SemaphoreType.DMA,
            pltpu.SemaphoreType.DMA((8,)),
            pltpu.SemaphoreType.DMA((8,)),
        ],
        compiler_params=ROOM,
        name="pick",
    )(send_list, voltage)

    arrived = lax.all_to_all(outgoing.reshape(peers, half, lanes), ("node", "freq"), 0, 0, tiled=True)

    start = lax.axis_index("freq") * tr_local
    index = lax.dynamic_slice_in_dim(model_index, start, tr_local)
    slot_grid = lax.dynamic_slice_in_dim(term_slot, start, tr_local, axis=1)
    batches = tr_local // BATCH
    index = index.reshape(BATCH, batches).T.reshape(-1)
    slot_list = slot_grid.reshape(-1)
    slot_grid = slot_grid.reshape(4 * BATCH // TEAM, TEAM, batches)
    tr_first, tr_seen = split_repeats(slot_grid, 1, senders * slots)
    tr_first = tr_first.reshape(-1)
    tr_flags = jnp.any(tr_seen, axis=(0, 1))
    tr_flags = jnp.concatenate([tr_flags, jnp.any(tr_flags.reshape(-1, STEP // BATCH), axis=1)]).astype(jnp.int32)
    send_grid = send_list.reshape(peers // TEAM, TEAM, slots)
    send_first, send_seen = split_repeats(send_grid, 1, nodes)
    send_first = send_first.reshape(-1)
    send_flags = jnp.any(send_seen.reshape(peers // BATCH, BATCH, 2, half), axis=(1, 2))
    send_flags = jnp.concatenate(
        [
            send_flags.reshape(-1),
            jnp.any(send_flags.reshape(peers // BATCH, 8, half // 8), axis=2).reshape(-1),
            jnp.any(send_flags, axis=1),
        ]
    ).astype(jnp.int32)
    cards = jnp.concatenate([model_table[:2], 1.0 / (1.0 + model_table[2:3]), model_table[3:]], axis=0)
    onehot = (index[:, None] == jnp.arange(cards.shape[1], dtype=jnp.int32)[None, :]).astype(F32)
    params = jnp.dot(onehot, cards.T, precision=HIGH)

    synthesis, analysis, slope_table = dft_tables(lanes)
    syn = np.zeros((2, 2, rows, 2, lanes))
    for f in range(2):
        for q in range(2):
            syn[f, q, :, q, :] = synthesis.T[f * rows : (f + 1) * rows]
    none = np.zeros((lanes, lanes))
    ana = np.concatenate(
        [np.block([[analysis.T, none], [none, slope_table.T]]), np.block([[slope_table.T, none], [none, slope_table.T]])],
        axis=1,
    )
    syn = split_weights(syn.reshape(2 * lanes, 2 * lanes))
    ana = split_weights(ana)

    returned = pl.pallas_call(
        device_kernel,
        out_shape=jax.ShapeDtypeStruct((senders, 2, half, lanes), F32),
        in_specs=[ANY] * 7,
        out_specs=ANY,
        scratch_shapes=[pltpu.SMEM(a.shape, a.dtype) for a in (slot_list, tr_first, tr_flags)]
        + [pltpu.VMEM(a.shape, a.dtype) for a in (params, syn, ana)]
        + [
            pltpu.VMEM((senders, 2, half, lanes), F32),
            pltpu.VMEM((senders * slots, lanes), F32),
        ]
        + [pltpu.VMEM((4, STEP, lanes), F32)] * 2
        + [pltpu.VMEM((STEP, 4 * lanes), F32)] * 2
        + [pltpu.VMEM((4, STEP, lanes), F32)] * 2
        + [pltpu.VMEM((senders * slots + 8, lanes), F32)] * 4
        + [pltpu.SemaphoreType.DMA((8,))] * 3,
        compiler_params=ROOM,
        name="devices",
    )(slot_list, tr_first, tr_flags, params, syn, ana, arrived.reshape(senders, 2, half, lanes))

    incoming = lax.all_to_all(returned.reshape(peers, half, lanes), ("node", "freq"), 0, 0, tiled=True)

    return pl.pallas_call(
        lambda *refs: residual_kernel(rows, slots, *refs),
        out_shape=jax.ShapeDtypeStruct((rows, nodes), F32),
        in_specs=[ANY] * 6,
        out_specs=ANY,
        scratch_shapes=[pltpu.SMEM(a.shape, a.dtype) for a in (send_list, send_first, send_flags)]
        + [pltpu.VMEM((1, nodes), F32), pltpu.VMEM((peers * half, lanes), F32), pltpu.VMEM((rows, nodes), F32)]
        + [pltpu.VMEM((nodes + 8, lanes), F32)] * 4
        + [
            pltpu.SemaphoreType.DMA((4,)),
            pltpu.SemaphoreType.DMA((8,)),
            pltpu.SemaphoreType.DMA,
            pltpu.SemaphoreType.DMA((8,)),
        ],
        compiler_params=ROOM,
        name="residual",
    )(send_list, send_first, send_flags, node_cond.reshape(1, nodes), incoming.reshape(peers * half, lanes), voltage)


def solution(mesh):
    return jax.shard_map(
        per_device,
        mesh=mesh,
        in_specs=(
            P("freq", "node"),
            P("node"),
            P(),
            P("node"),
            P("node", None, None, None),
            P(None, "node"),
        ),
        out_specs=P("freq", "node"),
        check_vma=False,
    )
```

```python
import jax
import jax.numpy as jnp
import numpy as np
from jax import lax
from jax.experimental import pallas as pl
from jax.experimental.pallas import tpu as pltpu
from jax.sharding import PartitionSpec as P

OMEGA = 0.05
HIGH = lax.Precision.HIGHEST
F32 = jnp.float32
BF16 = jnp.bfloat16
BATCH = 16
TEAM = 4
STEP = 128


def dft_tables(npoints):
    half_len = npoints // 2
    time_idx = np.arange(npoints)[:, None]
    row_idx = np.arange(npoints)[None, :]
    is_sine = (row_idx >= half_len) & (row_idx < npoints - 1)
    edge_row = (row_idx == 0) | (row_idx == npoints - 1)
    harmonic = np.where(row_idx < half_len, row_idx, np.where(row_idx == npoints - 1, half_len, row_idx - half_len + 1))
    phases = 2.0 * np.pi / npoints * (time_idx * harmonic % npoints)
    basis_rows = np.where(is_sine, np.sin(phases), np.cos(phases))
    weight = np.where(edge_row, 1.0 / npoints, 2.0 / npoints)
    deriv_rate = OMEGA * harmonic * weight
    slope_rows = np.where(is_sine, -deriv_rate * np.cos(phases), np.where(edge_row, 0.0, deriv_rate * np.sin(phases)))
    return basis_rows, (weight * basis_rows).T, slope_rows.T


def split_weights(w):
    w = w.astype(np.float32)
    hi = w.astype(jnp.bfloat16)
    lo = (w - hi.astype(np.float32)).astype(jnp.bfloat16)
    return jnp.asarray(np.concatenate([hi, lo, hi], axis=0))


def dot3(x, w3):
    hi = x.astype(BF16)
    lo = (x - hi.astype(F32)).astype(BF16)
    return jnp.dot(jnp.concatenate([hi, hi, lo], axis=1), w3, preferred_element_type=F32)


def soft_bend(values):
    return values + 0.5 * jnp.tanh(values)


def softplus(x):
    return jnp.maximum(x, 0.0) + jnp.log1p(jnp.exp(-jnp.abs(x)))


def pick_kernel(rows, slots, idx_hbm, v_hbm, out_hbm, idx, vbuf, table, obuf, idx_sem, in_sem, out_sem):
    nodes = vbuf.shape[1]
    n_in = in_sem.shape[0]
    n_out = out_sem.shape[0]
    width = nodes // n_in
    half = slots // 2
    peers = obuf.shape[0] // half
    per_out = peers // n_out

    def fetch(c):
        cols = pl.ds(c * width, width)
        return pltpu.make_async_copy(v_hbm.at[:, cols], vbuf.at[:, cols], in_sem.at[c])

    def ship(c):
        part = pl.ds(c * per_out * half, per_out * half)
        return pltpu.make_async_copy(obuf.at[part], out_hbm.at[part], out_sem.at[c])

    for c in range(n_in):
        fetch(c).start()
    idx_copy = pltpu.make_async_copy(idx_hbm, idx, idx_sem)
    idx_copy.start()
    table[pl.ds(nodes, 8), :] = jnp.zeros((8, 128), F32)
    low = lax.broadcasted_iota(jnp.int32, (128, 128), 1) < rows
    for c in range(n_in):
        fetch(c).wait()

        def turn(b, carry, c=c):
            for w in range(8):
                at = pl.multiple_of(c * width + (b * 8 + w) * 256, 256)
                x = jnp.concatenate([vbuf[:, pl.ds(at, 128)], vbuf[:, pl.ds(at + 128, 128)]], axis=0).T
                y = pltpu.roll(x, rows, 1)
                table[pl.ds(at, 128), :] = jnp.where(low, x, y)
                table[pl.ds(at + 128, 128), :] = jnp.where(low, y, x)
            return carry

        lax.fori_loop(0, width // 2048, turn, 0)
    idx_copy.wait()

    for c in range(n_out):

        def rounds(i, carry, c=c):
            for w in range(8):
                j = i * 8 + w
                for p in range(c * per_out, (c + 1) * per_out):
                    a = table[pl.ds(idx.at[pl.ds(p * slots, half)][j], 1), :]
                    b = table[pl.ds(idx.at[pl.ds(p * slots + half, half)][j], 1), :]
                    obuf.at[pl.ds(p * half, half)][pl.ds(j, 1), :] = jnp.where(low[:1], a, b)
            return carry

        lax.fori_loop(0, half // 8, rounds, 0)
        ship(c).start()
    for c in range(n_out):
        ship(c).wait()


def add_rows(table, names, rows):
    spots = [pl.ds(name, 1) for name in names]
    sums = [table[spot, :] + row for spot, row in zip(spots, rows)]
    for spot, total in zip(spots, sums):
        table[spot, :] = total


def device_kernel(
    idx_hbm, first_hbm, flags_hbm, params_hbm, syn_hbm, ana_hbm, x_hbm, out_hbm,
    idx, first, flags, params, syn, ana,
    xbuf, wave, volts0, volts1, duo0, duo1, amps0, amps1, acc0, acc1, acc2, acc3, own_sem, in_sem, out_sem,
):
    accs = (acc0, acc1, acc2, acc3)
    volts, duos, amps = (volts0, volts1), (duo0, duo1), (amps0, amps1)
    senders, _, half, lanes = xbuf.shape
    n_in = in_sem.shape[0]
    n_out = out_sem.shape[0]
    per_in = senders // n_in
    per_out = senders // n_out
    tr_local = params.shape[0]
    batches = tr_local // BATCH
    step = volts0.shape[1]
    inner = step // BATCH
    steps = tr_local // step
    spare = wave.shape[0]

    def fetch(c):
        part = pl.ds(c * per_in, per_in)
        return pltpu.make_async_copy(x_hbm.at[part], xbuf.at[part], in_sem.at[c])

    def ship(c):
        part = pl.ds(c * per_out, per_out)
        return pltpu.make_async_copy(xbuf.at[part], out_hbm.at[part], out_sem.at[c])

    own = [
        pltpu.make_async_copy(source, copy, own_sem.at[i])
        for i, (source, copy) in enumerate(
            [
                (syn_hbm, syn), (idx_hbm, idx), (params_hbm, params),
                (ana_hbm, ana), (first_hbm, first), (flags_hbm, flags),
            ]
        )
    ]
    for copy in own[:1]:
        copy.start()
    for c in range(n_in):
        fetch(c).start()
    for copy in own[1:]:
        copy.start()
    for copy in own[:1]:
        copy.wait()
    rows_in = per_in * 2 * half

    def synth(c, carry):
        at = pl.multiple_of(c * rows_in, rows_in)
        for acc in accs:
            acc[pl.ds(at, rows_in), :] = jnp.zeros((rows_in, lanes), F32)
        fetch(c).wait()
        x = xbuf[pl.ds(c * per_in, per_in)]
        xx = jnp.concatenate(
            [x[:, 0].reshape(per_in * half, lanes), x[:, 1].reshape(per_in * half, lanes)], axis=1
        )
        y = jnp.concatenate([dot3(part, syn[...]) for part in jnp.split(xx, 2, axis=0)], axis=0)
        for s in range(per_in):
            wave[pl.ds(at + s * 2 * half, half), :] = y[s * half : (s + 1) * half, :lanes]
            wave[pl.ds(at + (s * 2 + 1) * half, half), :] = y[s * half : (s + 1) * half, lanes:]
        return carry

    lax.fori_loop(0, n_in, synth, 0)
    for copy in own[1:]:
        copy.wait()

    def names_of(source, k, b):
        return [source.at[pl.ds((k * BATCH + u) * batches, batches)][b] for u in range(BATCH)]

    def collect(buf, i, q):
        for k in range(4):
            for u, name in enumerate(names_of(idx, k, i * inner + q)):
                buf[k, q * BATCH + u : q * BATCH + u + 1, :] = wave[pl.ds(name, 1), :]

    def model(buf, duo, i, q):
        at = pl.ds(q * BATCH, BATCH)
        par = params[pl.ds(pl.multiple_of(i * step + q * BATCH, BATCH), BATCH), :]
        thresh, strength, inv_slope, cap_gs, cap_gd, cap_db = (par[:, m : m + 1] for m in range(6))
        drain, gate, source, bulk = (buf[k, at, :] for k in range(4))
        pinch = (gate - thresh) * inv_slope
        forward = softplus(0.5 * (pinch - source))
        reverse = softplus(0.5 * (pinch - drain))
        duo[at, 0:lanes] = strength * (forward * forward - reverse * reverse)
        duo[at, lanes : 2 * lanes] = cap_gs * soft_bend(gate - source)
        duo[at, 2 * lanes : 3 * lanes] = cap_gd * soft_bend(gate - drain)
        duo[at, 3 * lanes : 4 * lanes] = cap_db * soft_bend(drain - bulk)

    def analyse(duo, amp):
        left = dot3(duo[:, : 2 * lanes], ana[:, : 2 * lanes])
        right = dot3(duo[:, 2 * lanes :], ana[:, 2 * lanes :])
        chan, gs = left[:, :lanes], left[:, lanes:]
        gd, db = right[:, :lanes], right[:, lanes:]
        amp[0] = chan + (db - gd)
        amp[1] = gs + gd
        amp[2] = -chan - gs
        amp[3] = -db

    def spread(amp, i, q):
        names = [names_of(first, k, i * inner + q) for k in range(4)]
        for team in range(0, BATCH, TEAM):
            for k in range(4):
                at = q * BATCH + team
                add_rows(
                    accs[k],
                    names[k][team : team + TEAM],
                    [amp[k, at + u : at + u + 1, :] for u in range(TEAM)],
                )

    def repeat(amp, i):
        def batch(n, carry):
            q = flags[steps + i * inner + n]
            b = i * inner + q
            for u in range(BATCH):
                for k in range(4):
                    at = (k * BATCH + u) * batches + b
                    spot = pl.ds(jnp.where(first[at] == spare, idx[at], spare), 1)
                    accs[k][spot, :] = accs[k][spot, :] + amp[k, pl.ds(q * BATCH + u, 1), :]
            return carry

        lax.fori_loop(0, flags[i], batch, 0)

    def stage(i, w, *, ahead=None, now=True, before=True, late=None):
        if before:
            analyse(duos[1 - w], amps[1 - w])
        for q in range(inner):
            if ahead is not None:
                collect(volts[1 - w], ahead, q)
            if now:
                model(volts[w], duos[w], i, q)
            if late is not None:
                spread(amps[w], late, q)
        if late is not None:
            repeat(amps[w], late)

    for q in range(inner):
        collect(volts0, 0, q)
    stage(0, 0, ahead=1, before=False)
    stage(1, 1, ahead=2)

    def pair(j, carry):
        for w in range(2):
            i = 2 * j + w
            stage(i, w, ahead=jnp.minimum(i + 1, steps - 1), late=i - 2)
        return carry

    lax.fori_loop(1, steps // 2, pair, 0)
    stage(steps, 0, now=False, late=steps - 2)
    stage(steps + 1, 1, now=False, before=False, late=steps - 1)
    low = lax.broadcasted_iota(jnp.int32, (half, lanes), 1) < half

    def pack(c, carry):
        for s in range(per_out):
            peer = c * per_out + s
            at = pl.multiple_of(peer * 2 * half, 2 * half)
            upper = pl.ds(at + half, half)
            at = pl.ds(at, half)
            one = sum(acc[at, :] for acc in accs)
            two = sum(acc[upper, :] for acc in accs)
            xbuf[peer, 0] = jnp.where(low, one, pltpu.roll(two, half, 1))
            xbuf[peer, 1] = jnp.where(low, pltpu.roll(one, half, 1), two)
        ship(c).start()
        return carry

    lax.fori_loop(0, n_out, pack, 0)
    for c in range(n_out):
        ship(c).wait()


def residual_kernel(
    rows, slots, idx_hbm, first_hbm, flags_hbm, cond_hbm, x_hbm, v_hbm, out_hbm,
    idx, first, flags, cond, xbuf, vbuf, low0, high0, low1, high1, own_sem, in_sem, v_sem, out_sem,
):
    nodes = vbuf.shape[1]
    half = slots // 2
    n_in = in_sem.shape[0]
    n_out = out_sem.shape[0]
    width = nodes // n_out
    peers = xbuf.shape[0] // half
    per_in = peers // n_in

    def fetch(c):
        part = pl.ds(c * per_in * half, per_in * half)
        return pltpu.make_async_copy(x_hbm.at[part], xbuf.at[part], in_sem.at[c])

    def ship(c):
        cols = pl.ds(c * width, width)
        return pltpu.make_async_copy(vbuf.at[:, cols], out_hbm.at[:, cols], out_sem.at[c])

    v_copy = pltpu.make_async_copy(v_hbm, vbuf, v_sem)
    own = [
        pltpu.make_async_copy(source, copy, own_sem.at[i])
        for i, (source, copy) in enumerate([(first_hbm, first), (flags_hbm, flags), (idx_hbm, idx), (cond_hbm, cond)])
    ]
    own[0].start()
    fetch(0).start()
    for copy in own[1:]:
        copy.start()
    for c in range(1, n_in):
        fetch(c).start()
    v_copy.start()

    def clear(i, carry):
        for acc in (low0, high0, low1, high1):
            acc[pl.ds(pl.multiple_of(i * 256, 256), 256), :] = jnp.zeros((256, 128), F32)
        return carry

    lax.fori_loop(0, nodes // 256, clear, 0)

    tables = ((low0, high0), (low1, high1))
    for copy in own:
        copy.wait()

    for c in range(n_in):
        fetch(c).wait()
        mine = range(c * per_in, (c + 1) * per_in)

        def slot_group(i, carry, mine=mine):
            for w in range(8):
                for team in range(0, BATCH, TEAM):
                    for h in range(2):
                        team_of = mine[team : team + TEAM]
                        add_rows(
                            tables[(team // TEAM) % 2][h],
                            [first.at[pl.ds(p * slots + h * half, half)][i * 8 + w] for p in team_of],
                            [xbuf.at[pl.ds(p * half, half)][pl.ds(i * 8 + w, 1), :] for p in team_of],
                        )
            return carry

        lax.fori_loop(0, half // 8, slot_group, 0)

        def repeat(n, carry, c=c, mine=mine):
            i = flags[n_in + c * half + n]
            for q in range(BATCH):
                x = xbuf[pl.ds(mine[q] * half + i, 1), :]
                for h in range(2):
                    at = mine[q] * slots + h * half + i
                    spot = pl.ds(jnp.where(first[at] == nodes, idx[at], nodes), 1)
                    table = tables[q % 2][h]
                    table[spot, :] = table[spot, :] + x
            return carry

        lax.fori_loop(0, flags[c], repeat, 0)

    v_copy.wait()
    low = lax.broadcasted_iota(jnp.int32, (128, 128), 1) < rows

    def finish(c, carry):
        def turn(b, carry):
            for w in range(8):
                at = pl.multiple_of(c * width + (b * 8 + w) * 256, 256)
                one, two = pl.ds(at, 128), pl.ds(at + 128, 128)
                both = jnp.where(low, low0[one, :] + low1[one, :], high0[two, :] + high1[two, :])
                both = both + pltpu.roll(jnp.where(low, low0[two, :] + low1[two, :], high0[one, :] + high1[one, :]), rows, 1)
                both = both.T
                vbuf[:, one] = vbuf[:, one] * cond[:, one] + both[:rows]
                vbuf[:, two] = vbuf[:, two] * cond[:, two] + both[rows:]
            return carry

        lax.fori_loop(0, width // 2048, turn, 0)
        ship(c).start()
        return carry

    lax.fori_loop(0, n_out, finish, 0)
    for c in range(n_out):
        ship(c).wait()


def split_repeats(names, axis, spare):
    columns = [lax.index_in_dim(names, i, axis, keepdims=False) for i in range(names.shape[axis])]
    seen = [jnp.zeros(columns[0].shape, jnp.bool_)]
    for i in range(1, len(columns)):
        hit = columns[i] == columns[0]
        for j in range(1, i):
            hit = hit | (columns[i] == columns[j])
        seen.append(hit)
    seen = jnp.stack(seen, axis) & (names != spare)
    return jnp.where(seen, spare, names), seen


def marked(flags):
    n = flags.shape[1]
    place = jnp.arange(n, dtype=jnp.int32)
    rank = jnp.sum((flags[:, None, :] & (place[None, None, :] < place[None, :, None])).astype(jnp.int32), axis=2)
    hit = flags[:, None, :] & (rank[:, None, :] == place[None, :, None])
    order = jnp.sum(jnp.where(hit, place[None, None, :], 0), axis=2)
    return jnp.concatenate([jnp.sum(flags.astype(jnp.int32), axis=1), order.reshape(-1)])


ANY = pl.BlockSpec(memory_space=pl.ANY)
ROOM = pltpu.CompilerParams(vmem_limit_bytes=60 * 2**20)


def per_device(voltage, node_cond, model_table, model_index, send_nodes, term_slot):
    rows, nodes = voltage.shape
    senders = send_nodes.shape[1]
    groups = send_nodes.shape[2]
    slots = send_nodes.shape[3]
    half = slots // 2
    peers = senders * groups
    lanes = rows * groups
    tr_local = term_slot.shape[1] // groups
    send_list = send_nodes.reshape(-1)

    outgoing = pl.pallas_call(
        lambda *refs: pick_kernel(rows, slots, *refs),
        out_shape=jax.ShapeDtypeStruct((peers * half, lanes), F32),
        in_specs=[ANY, ANY],
        out_specs=ANY,
        scratch_shapes=[
            pltpu.SMEM((peers * slots,), jnp.int32),
            pltpu.VMEM((rows, nodes), F32),
            pltpu.VMEM((nodes + 8, lanes), F32),
            pltpu.VMEM((peers * half, lanes), F32),
            pltpu.SemaphoreType.DMA,
            pltpu.SemaphoreType.DMA((8,)),
            pltpu.SemaphoreType.DMA((8,)),
        ],
        compiler_params=ROOM,
        name="pick",
    )(send_list, voltage)

    arrived = lax.all_to_all(outgoing.reshape(peers, half, lanes), ("node", "freq"), 0, 0, tiled=True)

    start = lax.axis_index("freq") * tr_local
    index = lax.dynamic_slice_in_dim(model_index, start, tr_local)
    slot_grid = lax.dynamic_slice_in_dim(term_slot, start, tr_local, axis=1)
    batches = tr_local // BATCH
    index = index.reshape(BATCH, batches).T.reshape(-1)
    slot_list = slot_grid.reshape(-1)
    slot_grid = slot_grid.reshape(4 * BATCH // TEAM, TEAM, batches)
    tr_first, tr_seen = split_repeats(slot_grid, 1, senders * slots)
    tr_first = tr_first.reshape(-1)
    tr_flags = marked(jnp.any(tr_seen, axis=(0, 1)).reshape(-1, STEP // BATCH))
    send_grid = send_list.reshape(peers // TEAM, TEAM, slots)
    send_first, send_seen = split_repeats(send_grid, 1, nodes)
    send_first = send_first.reshape(-1)
    send_flags = jnp.any(send_seen.reshape(peers // BATCH, BATCH, 2, half), axis=(1, 2))
    send_flags = marked(send_flags)
    cards = jnp.concatenate([model_table[:2], 1.0 / (1.0 + model_table[2:3]), model_table[3:]], axis=0)
    onehot = (index[:, None] == jnp.arange(cards.shape[1], dtype=jnp.int32)[None, :]).astype(F32)
    params = jnp.dot(onehot, cards.T, precision=HIGH)

    synthesis, analysis, slope_table = dft_tables(lanes)
    syn = np.zeros((2, 2, rows, 2, lanes))
    for f in range(2):
        for q in range(2):
            syn[f, q, :, q, :] = synthesis.T[f * rows : (f + 1) * rows]
    none = np.zeros((lanes, lanes))
    ana = np.concatenate(
        [np.block([[analysis.T, none], [none, slope_table.T]]), np.block([[slope_table.T, none], [none, slope_table.T]])],
        axis=1,
    )
    syn = split_weights(syn.reshape(2 * lanes, 2 * lanes))
    ana = split_weights(ana)

    returned = pl.pallas_call(
        device_kernel,
        out_shape=jax.ShapeDtypeStruct((senders, 2, half, lanes), F32),
        in_specs=[ANY] * 7,
        out_specs=ANY,
        scratch_shapes=[pltpu.SMEM(a.shape, a.dtype) for a in (slot_list, tr_first, tr_flags)]
        + [pltpu.VMEM(a.shape, a.dtype) for a in (params, syn, ana)]
        + [
            pltpu.VMEM((senders, 2, half, lanes), F32),
            pltpu.VMEM((senders * slots, lanes), F32),
        ]
        + [pltpu.VMEM((4, STEP, lanes), F32)] * 2
        + [pltpu.VMEM((STEP, 4 * lanes), F32)] * 2
        + [pltpu.VMEM((4, STEP, lanes), F32)] * 2
        + [pltpu.VMEM((senders * slots + 8, lanes), F32)] * 4
        + [pltpu.SemaphoreType.DMA((8,))] * 3,
        compiler_params=ROOM,
        name="devices",
    )(slot_list, tr_first, tr_flags, params, syn, ana, arrived.reshape(senders, 2, half, lanes))

    incoming = lax.all_to_all(returned.reshape(peers, half, lanes), ("node", "freq"), 0, 0, tiled=True)

    return pl.pallas_call(
        lambda *refs: residual_kernel(rows, slots, *refs),
        out_shape=jax.ShapeDtypeStruct((rows, nodes), F32),
        in_specs=[ANY] * 6,
        out_specs=ANY,
        scratch_shapes=[pltpu.SMEM(a.shape, a.dtype) for a in (send_list, send_first, send_flags)]
        + [pltpu.VMEM((1, nodes), F32), pltpu.VMEM((peers * half, lanes), F32), pltpu.VMEM((rows, nodes), F32)]
        + [pltpu.VMEM((nodes + 8, lanes), F32)] * 4
        + [
            pltpu.SemaphoreType.DMA((4,)),
            pltpu.SemaphoreType.DMA((8,)),
            pltpu.SemaphoreType.DMA,
            pltpu.SemaphoreType.DMA((8,)),
        ],
        compiler_params=ROOM,
        name="residual",
    )(send_list, send_first, send_flags, node_cond.reshape(1, nodes), incoming.reshape(peers * half, lanes), voltage)


def solution(mesh):
    return jax.shard_map(
        per_device,
        mesh=mesh,
        in_specs=(
            P("freq", "node"),
            P("node"),
            P(),
            P("node"),
            P("node", None, None, None),
            P(None, "node"),
        ),
        out_specs=P("freq", "node"),
        check_vma=False,
    )
```

```python
import jax
import jax.numpy as jnp
import numpy as np
from jax import lax
from jax.experimental import pallas as pl
from jax.experimental.pallas import tpu as pltpu
from jax.sharding import PartitionSpec as P

OMEGA = 0.05
HIGH = lax.Precision.HIGHEST
F32 = jnp.float32
BF16 = jnp.bfloat16
BATCH = 16
TEAM = 4
STEP = 128


def dft_tables(npoints):
    half_len = npoints // 2
    time_idx = np.arange(npoints)[:, None]
    row_idx = np.arange(npoints)[None, :]
    is_sine = (row_idx >= half_len) & (row_idx < npoints - 1)
    edge_row = (row_idx == 0) | (row_idx == npoints - 1)
    harmonic = np.where(row_idx < half_len, row_idx, np.where(row_idx == npoints - 1, half_len, row_idx - half_len + 1))
    phases = 2.0 * np.pi / npoints * (time_idx * harmonic % npoints)
    basis_rows = np.where(is_sine, np.sin(phases), np.cos(phases))
    weight = np.where(edge_row, 1.0 / npoints, 2.0 / npoints)
    deriv_rate = OMEGA * harmonic * weight
    slope_rows = np.where(is_sine, -deriv_rate * np.cos(phases), np.where(edge_row, 0.0, deriv_rate * np.sin(phases)))
    return basis_rows, (weight * basis_rows).T, slope_rows.T


def split_weights(w):
    w = w.astype(np.float32)
    hi = w.astype(jnp.bfloat16)
    lo = (w - hi.astype(np.float32)).astype(jnp.bfloat16)
    return jnp.asarray(np.concatenate([hi, lo, hi], axis=0))


def dot3(x, w3):
    hi = x.astype(BF16)
    lo = (x - hi.astype(F32)).astype(BF16)
    return jnp.dot(jnp.concatenate([hi, hi, lo], axis=1), w3, preferred_element_type=F32)


def soft_bend(values):
    return values + 0.5 * jnp.tanh(values)


def softplus(x):
    return jnp.maximum(x, 0.0) + jnp.log1p(jnp.exp(-jnp.abs(x)))


def pick_kernel(rows, slots, idx_hbm, v_hbm, out_hbm, idx, vbuf, table, obuf, idx_sem, in_sem, out_sem):
    nodes = vbuf.shape[1]
    n_in = in_sem.shape[0]
    n_out = out_sem.shape[0]
    width = nodes // n_in
    half = slots // 2
    peers = obuf.shape[0] // half
    per_out = peers // n_out

    def fetch(c):
        cols = pl.ds(c * width, width)
        return pltpu.make_async_copy(v_hbm.at[:, cols], vbuf.at[:, cols], in_sem.at[c])

    def ship(c):
        part = pl.ds(c * per_out * half, per_out * half)
        return pltpu.make_async_copy(obuf.at[part], out_hbm.at[part], out_sem.at[c])

    for c in range(n_in):
        fetch(c).start()
    idx_copy = pltpu.make_async_copy(idx_hbm, idx, idx_sem)
    idx_copy.start()
    table[pl.ds(nodes, 8), :] = jnp.zeros((8, 128), F32)
    low = lax.broadcasted_iota(jnp.int32, (128, 128), 1) < rows
    def turn(c, carry):
        fetch(c).wait()
        for w in range(width // 256):
            at = pl.multiple_of(c * width + w * 256, 256)
            x = jnp.concatenate([vbuf[:, pl.ds(at, 128)], vbuf[:, pl.ds(at + 128, 128)]], axis=0).T
            y = pltpu.roll(x, rows, 1)
            table[pl.ds(at, 128), :] = jnp.where(low, x, y)
            table[pl.ds(at + 128, 128), :] = jnp.where(low, y, x)
        return carry

    lax.fori_loop(0, n_in, turn, 0)
    idx_copy.wait()

    def tail(ref, offset):
        return ref.at[pl.ds(offset, ref.shape[0] - offset)]

    def group(c, carry):
        def rounds(i, carry):
            for w in range(16):
                j = i * 16 + w
                name, out = c * (per_out * slots) + j, c * (per_out * half) + j
                for p in range(per_out):
                    a = table[pl.ds(tail(idx, p * slots)[name], 1), :]
                    b = table[pl.ds(tail(idx, p * slots + half)[name], 1), :]
                    tail(obuf, p * half)[pl.ds(out, 1), :] = jnp.where(low[:1], a, b)
            return carry

        lax.fori_loop(0, half // 16, rounds, 0)
        ship(c).start()
        return carry

    lax.fori_loop(0, n_out, group, 0)
    for c in range(n_out):
        ship(c).wait()


def add_rows(table, names, rows):
    spots = [pl.ds(name, 1) for name in names]
    sums = [table[spot, :] + row for spot, row in zip(spots, rows)]
    for spot, total in zip(spots, sums):
        table[spot, :] = total


def device_kernel(
    idx_hbm, first_hbm, flags_hbm, params_hbm, syn_hbm, ana_hbm, x_hbm, out_hbm,
    idx, first, flags, params, syn, ana,
    xbuf, wave, volts0, volts1, duo0, duo1, amps0, amps1, acc0, acc1, acc2, acc3, own_sem, in_sem, out_sem,
):
    accs = (acc0, acc1, acc2, acc3)
    volts, duos, amps = (volts0, volts1), (duo0, duo1), (amps0, amps1)
    senders, _, half, lanes = xbuf.shape
    n_in = in_sem.shape[0]
    n_out = out_sem.shape[0]
    per_in = senders // n_in
    per_out = senders // n_out
    tr_local = params.shape[0]
    batches = tr_local // BATCH
    step = volts0.shape[1]
    inner = step // BATCH
    steps = tr_local // step
    spare = wave.shape[0]

    def fetch(c):
        part = pl.ds(c * per_in, per_in)
        return pltpu.make_async_copy(x_hbm.at[part], xbuf.at[part], in_sem.at[c])

    def ship(c):
        part = pl.ds(c * per_out, per_out)
        return pltpu.make_async_copy(xbuf.at[part], out_hbm.at[part], out_sem.at[c])

    own = [
        pltpu.make_async_copy(source, copy, own_sem.at[i])
        for i, (source, copy) in enumerate(
            [
                (syn_hbm, syn), (idx_hbm, idx), (params_hbm, params),
                (ana_hbm, ana), (first_hbm, first), (flags_hbm, flags),
            ]
        )
    ]
    for copy in own[:1]:
        copy.start()
    for c in range(n_in):
        fetch(c).start()
    for copy in own[1:]:
        copy.start()
    for copy in own[:1]:
        copy.wait()
    rows_in = per_in * 2 * half

    def synth(c, carry):
        at = pl.multiple_of(c * rows_in, rows_in)
        for acc in accs:
            acc[pl.ds(at, rows_in), :] = jnp.zeros((rows_in, lanes), F32)
        fetch(c).wait()
        x = xbuf[pl.ds(c * per_in, per_in)]
        xx = jnp.concatenate(
            [x[:, 0].reshape(per_in * half, lanes), x[:, 1].reshape(per_in * half, lanes)], axis=1
        )
        y = jnp.concatenate([dot3(part, syn[...]) for part in jnp.split(xx, 2, axis=0)], axis=0)
        for s in range(per_in):
            wave[pl.ds(at + s * 2 * half, half), :] = y[s * half : (s + 1) * half, :lanes]
            wave[pl.ds(at + (s * 2 + 1) * half, half), :] = y[s * half : (s + 1) * half, lanes:]
        return carry

    lax.fori_loop(0, n_in, synth, 0)
    for copy in own[1:]:
        copy.wait()

    def names_of(source, k, b):
        return [source.at[pl.ds((k * BATCH + u) * batches, batches)][b] for u in range(BATCH)]

    def collect(buf, i, q):
        for k in range(4):
            for u, name in enumerate(names_of(idx, k, i * inner + q)):
                buf[k, q * BATCH + u : q * BATCH + u + 1, :] = wave[pl.ds(name, 1), :]

    def model(buf, duo, i, q):
        at = pl.ds(q * BATCH, BATCH)
        par = params[pl.ds(pl.multiple_of(i * step + q * BATCH, BATCH), BATCH), :]
        thresh, strength, inv_slope, cap_gs, cap_gd, cap_db = (par[:, m : m + 1] for m in range(6))
        drain, gate, source, bulk = (buf[k, at, :] for k in range(4))
        pinch = (gate - thresh) * inv_slope
        forward = softplus(0.5 * (pinch - source))
        reverse = softplus(0.5 * (pinch - drain))
        duo[at, 0:lanes] = strength * (forward * forward - reverse * reverse)
        duo[at, lanes : 2 * lanes] = cap_gs * soft_bend(gate - source)
        duo[at, 2 * lanes : 3 * lanes] = cap_gd * soft_bend(gate - drain)
        duo[at, 3 * lanes : 4 * lanes] = cap_db * soft_bend(drain - bulk)

    def analyse(duo, amp):
        left = dot3(duo[:, : 2 * lanes], ana[:, : 2 * lanes])
        right = dot3(duo[:, 2 * lanes :], ana[:, 2 * lanes :])
        chan, gs = left[:, :lanes], left[:, lanes:]
        gd, db = right[:, :lanes], right[:, lanes:]
        amp[0] = chan + (db - gd)
        amp[1] = gs + gd
        amp[2] = -chan - gs
        amp[3] = -db

    def spread(amp, i, q):
        names = [names_of(first, k, i * inner + q) for k in range(4)]
        for team in range(0, BATCH, TEAM):
            for k in range(4):
                at = q * BATCH + team
                add_rows(
                    accs[k],
                    names[k][team : team + TEAM],
                    [amp[k, at + u : at + u + 1, :] for u in range(TEAM)],
                )

    def repeat(amp, i):
        def batch(n, carry):
            q = flags[steps + i * inner + n]
            b = i * inner + q
            for u in range(BATCH):
                for k in range(4):
                    at = (k * BATCH + u) * batches + b
                    spot = pl.ds(jnp.where(first[at] == spare, idx[at], spare), 1)
                    accs[k][spot, :] = accs[k][spot, :] + amp[k, pl.ds(q * BATCH + u, 1), :]
            return carry

        lax.fori_loop(0, flags[i], batch, 0)

    def stage(i, w, *, ahead=None, now=True, before=True, late=None):
        if before:
            analyse(duos[1 - w], amps[1 - w])
        for q in range(inner):
            if ahead is not None:
                collect(volts[1 - w], ahead, q)
            if now:
                model(volts[w], duos[w], i, q)
            if late is not None:
                spread(amps[w], late, q)
        if late is not None:
            repeat(amps[w], late)

    for q in range(inner):
        collect(volts0, 0, q)
    stage(0, 0, ahead=1, before=False)
    stage(1, 1, ahead=2)

    def pair(j, carry):
        for w in range(2):
            i = 2 * j + w
            stage(i, w, ahead=jnp.minimum(i + 1, steps - 1), late=i - 2)
        return carry

    lax.fori_loop(1, steps // 2, pair, 0)
    stage(steps, 0, now=False, late=steps - 2)
    stage(steps + 1, 1, now=False, before=False, late=steps - 1)
    low = lax.broadcasted_iota(jnp.int32, (half, lanes), 1) < half

    def pack(c, carry):
        for s in range(per_out):
            peer = c * per_out + s
            at = pl.multiple_of(peer * 2 * half, 2 * half)
            upper = pl.ds(at + half, half)
            at = pl.ds(at, half)
            one = sum(acc[at, :] for acc in accs)
            two = sum(acc[upper, :] for acc in accs)
            xbuf[peer, 0] = jnp.where(low, one, pltpu.roll(two, half, 1))
            xbuf[peer, 1] = jnp.where(low, pltpu.roll(one, half, 1), two)
        ship(c).start()
        return carry

    lax.fori_loop(0, n_out, pack, 0)
    for c in range(n_out):
        ship(c).wait()


def residual_kernel(
    rows, slots, idx_hbm, first_hbm, flags_hbm, cond_hbm, x_hbm, v_hbm, out_hbm,
    idx, first, flags, cond, xbuf, vbuf, low0, high0, low1, high1, own_sem, in_sem, v_sem, out_sem,
):
    nodes = vbuf.shape[1]
    half = slots // 2
    n_in = in_sem.shape[0]
    n_out = out_sem.shape[0]
    width = nodes // n_out
    peers = xbuf.shape[0] // half
    per_in = peers // n_in

    def fetch(c):
        part = pl.ds(c * per_in * half, per_in * half)
        return pltpu.make_async_copy(x_hbm.at[part], xbuf.at[part], in_sem.at[c])

    def ship(c):
        cols = pl.ds(c * width, width)
        return pltpu.make_async_copy(vbuf.at[:, cols], out_hbm.at[:, cols], out_sem.at[c])

    v_copy = pltpu.make_async_copy(v_hbm, vbuf, v_sem)
    own = [
        pltpu.make_async_copy(source, copy, own_sem.at[i])
        for i, (source, copy) in enumerate([(first_hbm, first), (flags_hbm, flags), (idx_hbm, idx), (cond_hbm, cond)])
    ]
    own[0].start()
    fetch(0).start()
    for copy in own[1:]:
        copy.start()
    for c in range(1, n_in):
        fetch(c).start()
    v_copy.start()

    def clear(i, carry):
        for acc in (low0, high0, low1, high1):
            acc[pl.ds(pl.multiple_of(i * 256, 256), 256), :] = jnp.zeros((256, 128), F32)
        return carry

    lax.fori_loop(0, nodes // 256, clear, 0)

    tables = ((low0, high0), (low1, high1))
    for copy in own:
        copy.wait()

    def tail(ref, offset):
        return ref.at[pl.ds(offset, ref.shape[0] - offset)]

    def group(c, carry):
        fetch(c).wait()

        def slot_group(i, carry):
            for w in range(16):
                j = i * 16 + w
                name, row = c * (per_in * slots) + j, c * (per_in * half) + j
                for team in range(0, BATCH, TEAM):
                    for h in range(2):
                        add_rows(
                            tables[(team // TEAM) % 2][h],
                            [tail(first, q * slots + h * half)[name] for q in range(team, team + TEAM)],
                            [tail(xbuf, q * half)[pl.ds(row, 1), :] for q in range(team, team + TEAM)],
                        )
            return carry

        lax.fori_loop(0, half // 16, slot_group, 0)

        def repeat(n, carry):
            i = flags[n_in + c * half + n]
            for q in range(BATCH):
                p = c * per_in + q
                x = xbuf[pl.ds(p * half + i, 1), :]
                for h in range(2):
                    at = p * slots + h * half + i
                    spot = pl.ds(jnp.where(first[at] == nodes, idx[at], nodes), 1)
                    table = tables[q % 2][h]
                    table[spot, :] = table[spot, :] + x
            return carry

        lax.fori_loop(0, flags[c], repeat, 0)
        return carry

    lax.fori_loop(0, n_in, group, 0)
    v_copy.wait()
    low = lax.broadcasted_iota(jnp.int32, (128, 128), 1) < rows

    def finish(c, carry):
        def turn(b, carry):
            for w in range(8):
                at = pl.multiple_of(c * width + (b * 8 + w) * 256, 256)
                one, two = pl.ds(at, 128), pl.ds(at + 128, 128)
                both = jnp.where(low, low0[one, :] + low1[one, :], high0[two, :] + high1[two, :])
                both = both + pltpu.roll(jnp.where(low, low0[two, :] + low1[two, :], high0[one, :] + high1[one, :]), rows, 1)
                both = both.T
                vbuf[:, one] = vbuf[:, one] * cond[:, one] + both[:rows]
                vbuf[:, two] = vbuf[:, two] * cond[:, two] + both[rows:]
            return carry

        lax.fori_loop(0, width // 2048, turn, 0)
        ship(c).start()
        return carry

    lax.fori_loop(0, n_out, finish, 0)
    for c in range(n_out):
        ship(c).wait()


def split_repeats(names, axis, spare):
    columns = [lax.index_in_dim(names, i, axis, keepdims=False) for i in range(names.shape[axis])]
    seen = [jnp.zeros(columns[0].shape, jnp.bool_)]
    for i in range(1, len(columns)):
        hit = columns[i] == columns[0]
        for j in range(1, i):
            hit = hit | (columns[i] == columns[j])
        seen.append(hit)
    seen = jnp.stack(seen, axis) & (names != spare)
    return jnp.where(seen, spare, names), seen


def marked(flags):
    n = flags.shape[1]
    place = jnp.arange(n, dtype=jnp.int32)
    rank = jnp.sum((flags[:, None, :] & (place[None, None, :] < place[None, :, None])).astype(jnp.int32), axis=2)
    hit = flags[:, None, :] & (rank[:, None, :] == place[None, :, None])
    order = jnp.sum(jnp.where(hit, place[None, None, :], 0), axis=2)
    return jnp.concatenate([jnp.sum(flags.astype(jnp.int32), axis=1), order.reshape(-1)])


ANY = pl.BlockSpec(memory_space=pl.ANY)
ROOM = pltpu.CompilerParams(vmem_limit_bytes=60 * 2**20)


def per_device(voltage, node_cond, model_table, model_index, send_nodes, term_slot):
    rows, nodes = voltage.shape
    senders = send_nodes.shape[1]
    groups = send_nodes.shape[2]
    slots = send_nodes.shape[3]
    half = slots // 2
    peers = senders * groups
    lanes = rows * groups
    tr_local = term_slot.shape[1] // groups
    send_list = send_nodes.reshape(-1)

    outgoing = pl.pallas_call(
        lambda *refs: pick_kernel(rows, slots, *refs),
        out_shape=jax.ShapeDtypeStruct((peers * half, lanes), F32),
        in_specs=[ANY, ANY],
        out_specs=ANY,
        scratch_shapes=[
            pltpu.SMEM((peers * slots,), jnp.int32),
            pltpu.VMEM((rows, nodes), F32),
            pltpu.VMEM((nodes + 8, lanes), F32),
            pltpu.VMEM((peers * half, lanes), F32),
            pltpu.SemaphoreType.DMA,
            pltpu.SemaphoreType.DMA((8,)),
            pltpu.SemaphoreType.DMA((8,)),
        ],
        compiler_params=ROOM,
        name="pick",
    )(send_list, voltage)

    arrived = lax.all_to_all(outgoing.reshape(peers, half, lanes), ("node", "freq"), 0, 0, tiled=True)

    start = lax.axis_index("freq") * tr_local
    index = lax.dynamic_slice_in_dim(model_index, start, tr_local)
    slot_grid = lax.dynamic_slice_in_dim(term_slot, start, tr_local, axis=1)
    batches = tr_local // BATCH
    index = index.reshape(BATCH, batches).T.reshape(-1)
    slot_list = slot_grid.reshape(-1)
    slot_grid = slot_grid.reshape(4 * BATCH // TEAM, TEAM, batches)
    tr_first, tr_seen = split_repeats(slot_grid, 1, senders * slots)
    tr_first = tr_first.reshape(-1)
    tr_flags = marked(jnp.any(tr_seen, axis=(0, 1)).reshape(-1, STEP // BATCH))
    send_grid = send_list.reshape(peers // TEAM, TEAM, slots)
    send_first, send_seen = split_repeats(send_grid, 1, nodes)
    send_first = send_first.reshape(-1)
    send_flags = jnp.any(send_seen.reshape(peers // BATCH, BATCH, 2, half), axis=(1, 2))
    send_flags = marked(send_flags)
    cards = jnp.concatenate([model_table[:2], 1.0 / (1.0 + model_table[2:3]), model_table[3:]], axis=0)
    onehot = (index[:, None] == jnp.arange(cards.shape[1], dtype=jnp.int32)[None, :]).astype(F32)
    params = jnp.dot(onehot, cards.T, precision=HIGH)

    synthesis, analysis, slope_table = dft_tables(lanes)
    syn = np.zeros((2, 2, rows, 2, lanes))
    for f in range(2):
        for q in range(2):
            syn[f, q, :, q, :] = synthesis.T[f * rows : (f + 1) * rows]
    none = np.zeros((lanes, lanes))
    ana = np.concatenate(
        [np.block([[analysis.T, none], [none, slope_table.T]]), np.block([[slope_table.T, none], [none, slope_table.T]])],
        axis=1,
    )
    syn = split_weights(syn.reshape(2 * lanes, 2 * lanes))
    ana = split_weights(ana)

    returned = pl.pallas_call(
        device_kernel,
        out_shape=jax.ShapeDtypeStruct((senders, 2, half, lanes), F32),
        in_specs=[ANY] * 7,
        out_specs=ANY,
        scratch_shapes=[pltpu.SMEM(a.shape, a.dtype) for a in (slot_list, tr_first, tr_flags)]
        + [pltpu.VMEM(a.shape, a.dtype) for a in (params, syn, ana)]
        + [
            pltpu.VMEM((senders, 2, half, lanes), F32),
            pltpu.VMEM((senders * slots, lanes), F32),
        ]
        + [pltpu.VMEM((4, STEP, lanes), F32)] * 2
        + [pltpu.VMEM((STEP, 4 * lanes), F32)] * 2
        + [pltpu.VMEM((4, STEP, lanes), F32)] * 2
        + [pltpu.VMEM((senders * slots + 8, lanes), F32)] * 4
        + [pltpu.SemaphoreType.DMA((8,))] * 3,
        compiler_params=ROOM,
        name="devices",
    )(slot_list, tr_first, tr_flags, params, syn, ana, arrived.reshape(senders, 2, half, lanes))

    incoming = lax.all_to_all(returned.reshape(peers, half, lanes), ("node", "freq"), 0, 0, tiled=True)

    return pl.pallas_call(
        lambda *refs: residual_kernel(rows, slots, *refs),
        out_shape=jax.ShapeDtypeStruct((rows, nodes), F32),
        in_specs=[ANY] * 6,
        out_specs=ANY,
        scratch_shapes=[pltpu.SMEM(a.shape, a.dtype) for a in (send_list, send_first, send_flags)]
        + [pltpu.VMEM((1, nodes), F32), pltpu.VMEM((peers * half, lanes), F32), pltpu.VMEM((rows, nodes), F32)]
        + [pltpu.VMEM((nodes + 8, lanes), F32)] * 4
        + [
            pltpu.SemaphoreType.DMA((4,)),
            pltpu.SemaphoreType.DMA((8,)),
            pltpu.SemaphoreType.DMA,
            pltpu.SemaphoreType.DMA((8,)),
        ],
        compiler_params=ROOM,
        name="residual",
    )(send_list, send_first, send_flags, node_cond.reshape(1, nodes), incoming.reshape(peers * half, lanes), voltage)


def solution(mesh):
    return jax.shard_map(
        per_device,
        mesh=mesh,
        in_specs=(
            P("freq", "node"),
            P("node"),
            P(),
            P("node"),
            P("node", None, None, None),
            P(None, "node"),
        ),
        out_specs=P("freq", "node"),
        check_vma=False,
    )
```

```python
import jax
import jax.numpy as jnp
import numpy as np
from jax import lax
from jax.experimental import pallas as pl
from jax.experimental.pallas import tpu as pltpu
from jax.sharding import PartitionSpec as P

OMEGA = 0.05
HIGH = lax.Precision.HIGHEST
F32 = jnp.float32
BF16 = jnp.bfloat16
BATCH = 16
TEAM = 4
STEP = 128


def dft_tables(npoints):
    half_len = npoints // 2
    time_idx = np.arange(npoints)[:, None]
    row_idx = np.arange(npoints)[None, :]
    is_sine = (row_idx >= half_len) & (row_idx < npoints - 1)
    edge_row = (row_idx == 0) | (row_idx == npoints - 1)
    harmonic = np.where(row_idx < half_len, row_idx, np.where(row_idx == npoints - 1, half_len, row_idx - half_len + 1))
    phases = 2.0 * np.pi / npoints * (time_idx * harmonic % npoints)
    basis_rows = np.where(is_sine, np.sin(phases), np.cos(phases))
    weight = np.where(edge_row, 1.0 / npoints, 2.0 / npoints)
    deriv_rate = OMEGA * harmonic * weight
    slope_rows = np.where(is_sine, -deriv_rate * np.cos(phases), np.where(edge_row, 0.0, deriv_rate * np.sin(phases)))
    return basis_rows, (weight * basis_rows).T, slope_rows.T


def split_weights(w):
    w = w.astype(np.float32)
    hi = w.astype(jnp.bfloat16)
    lo = (w - hi.astype(np.float32)).astype(jnp.bfloat16)
    return jnp.asarray(np.concatenate([hi, lo, hi], axis=0))


def dot3(x, w3):
    hi = x.astype(BF16)
    lo = (x - hi.astype(F32)).astype(BF16)
    return jnp.dot(jnp.concatenate([hi, hi, lo], axis=1), w3, preferred_element_type=F32)


def soft_bend(values):
    return values + 0.5 * jnp.tanh(values)


def softplus(x):
    return jnp.maximum(x, 0.0) + jnp.log1p(jnp.exp(-jnp.abs(x)))


def pick_kernel(rows, slots, idx_hbm, v_hbm, out_hbm, idx, vbuf, table, obuf, idx_sem, in_sem, out_sem):
    nodes = vbuf.shape[1]
    n_in = in_sem.shape[0]
    n_out = out_sem.shape[0]
    width = nodes // n_in
    half = slots // 2
    peers = obuf.shape[0] // half
    per_out = peers // n_out

    def fetch(c):
        cols = pl.ds(c * width, width)
        return pltpu.make_async_copy(v_hbm.at[:, cols], vbuf.at[:, cols], in_sem.at[c])

    def ship(c):
        part = pl.ds(c * per_out * half, per_out * half)
        return pltpu.make_async_copy(obuf.at[part], out_hbm.at[part], out_sem.at[c])

    for c in range(n_in):
        fetch(c).start()
    idx_copy = pltpu.make_async_copy(idx_hbm, idx, idx_sem)
    idx_copy.start()
    table[pl.ds(nodes, 8), :] = jnp.zeros((8, 128), F32)
    low = lax.broadcasted_iota(jnp.int32, (128, 128), 1) < rows
    def turn(c, carry):
        fetch(c).wait()
        for w in range(width // 256):
            at = pl.multiple_of(c * width + w * 256, 256)
            x = jnp.concatenate([vbuf[:, pl.ds(at, 128)], vbuf[:, pl.ds(at + 128, 128)]], axis=0).T
            y = pltpu.roll(x, rows, 1)
            table[pl.ds(at, 128), :] = jnp.where(low, x, y)
            table[pl.ds(at + 128, 128), :] = jnp.where(low, y, x)
        return carry

    lax.fori_loop(0, n_in, turn, 0)
    idx_copy.wait()

    def tail(ref, offset):
        return ref.at[pl.ds(offset, ref.shape[0] - offset)]

    def group(c, carry):
        def rounds(i, carry):
            for w in range(16):
                j = i * 16 + w
                name, out = c * (per_out * slots) + j, c * (per_out * half) + j
                for p in range(per_out):
                    a = table[pl.ds(tail(idx, p * slots)[name], 1), :]
                    b = table[pl.ds(tail(idx, p * slots + half)[name], 1), :]
                    tail(obuf, p * half)[pl.ds(out, 1), :] = jnp.where(low[:1], a, b)
            return carry

        lax.fori_loop(0, half // 16, rounds, 0)
        ship(c).start()
        return carry

    lax.fori_loop(0, n_out, group, 0)
    for c in range(n_out):
        ship(c).wait()


def add_rows(table, names, rows):
    spots = [pl.ds(name, 1) for name in names]
    sums = [table[spot, :] + row for spot, row in zip(spots, rows)]
    for spot, total in zip(spots, sums):
        table[spot, :] = total


def device_kernel(
    idx_hbm, first_hbm, flags_hbm, params_hbm, syn_hbm, ana_hbm, x_hbm, out_hbm,
    idx, first, flags, params, syn, ana,
    xbuf, wave, volts0, volts1, duo0, duo1, amps0, amps1, acc0, acc1, acc2, acc3, own_sem, in_sem, out_sem,
):
    accs = (acc0, acc1, acc2, acc3)
    volts, duos, amps = (volts0, volts1), (duo0, duo1), (amps0, amps1)
    senders, _, half, lanes = xbuf.shape
    n_in = in_sem.shape[0]
    n_out = out_sem.shape[0]
    per_in = senders // n_in
    per_out = senders // n_out
    tr_local = params.shape[0]
    batches = tr_local // BATCH
    step = volts0.shape[1]
    inner = step // BATCH
    steps = tr_local // step
    spare = wave.shape[0]

    def fetch(c):
        part = pl.ds(c * per_in, per_in)
        return pltpu.make_async_copy(x_hbm.at[part], xbuf.at[part], in_sem.at[c])

    def ship(c):
        part = pl.ds(c * per_out, per_out)
        return pltpu.make_async_copy(xbuf.at[part], out_hbm.at[part], out_sem.at[c])

    own = [
        pltpu.make_async_copy(source, copy, own_sem.at[i])
        for i, (source, copy) in enumerate(
            [
                (syn_hbm, syn), (idx_hbm, idx), (params_hbm, params),
                (ana_hbm, ana), (first_hbm, first), (flags_hbm, flags),
            ]
        )
    ]
    for copy in own[:1]:
        copy.start()
    for c in range(n_in):
        fetch(c).start()
    for copy in own[1:]:
        copy.start()
    for copy in own[:1]:
        copy.wait()
    rows_in = per_in * 2 * half

    def synth(c, carry):
        at = pl.multiple_of(c * rows_in, rows_in)
        for acc in accs:
            acc[pl.ds(at, rows_in), :] = jnp.zeros((rows_in, lanes), F32)
        fetch(c).wait()
        x = xbuf[pl.ds(c * per_in, per_in)]
        xx = jnp.concatenate(
            [x[:, 0].reshape(per_in * half, lanes), x[:, 1].reshape(per_in * half, lanes)], axis=1
        )
        y = jnp.concatenate([dot3(part, syn[...]) for part in jnp.split(xx, 2, axis=0)], axis=0)
        for s in range(per_in):
            wave[pl.ds(at + s * 2 * half, half), :] = y[s * half : (s + 1) * half, :lanes]
            wave[pl.ds(at + (s * 2 + 1) * half, half), :] = y[s * half : (s + 1) * half, lanes:]
        return carry

    lax.fori_loop(0, n_in, synth, 0)
    for copy in own[1:]:
        copy.wait()

    def names_of(source, k, b):
        return [source.at[pl.ds((k * BATCH + u) * batches, batches)][b] for u in range(BATCH)]

    def collect(buf, i, q):
        for k in range(4):
            for u, name in enumerate(names_of(idx, k, i * inner + q)):
                buf[k, q * BATCH + u : q * BATCH + u + 1, :] = wave[pl.ds(name, 1), :]

    def model(buf, duo, i, q):
        at = pl.ds(q * BATCH, BATCH)
        par = params[pl.ds(pl.multiple_of(i * step + q * BATCH, BATCH), BATCH), :]
        thresh, strength, inv_slope, cap_gs, cap_gd, cap_db = (par[:, m : m + 1] for m in range(6))
        drain, gate, source, bulk = (buf[k, at, :] for k in range(4))
        pinch = (gate - thresh) * inv_slope
        forward = softplus(0.5 * (pinch - source))
        reverse = softplus(0.5 * (pinch - drain))
        duo[at, 0:lanes] = strength * (forward * forward - reverse * reverse)
        duo[at, lanes : 2 * lanes] = cap_gs * soft_bend(gate - source)
        duo[at, 2 * lanes : 3 * lanes] = cap_gd * soft_bend(gate - drain)
        duo[at, 3 * lanes : 4 * lanes] = cap_db * soft_bend(drain - bulk)

    def analyse(duo, amp):
        left = dot3(duo[:, : 2 * lanes], ana[:, : 2 * lanes])
        right = dot3(duo[:, 2 * lanes :], ana[:, 2 * lanes :])
        chan, gs = left[:, :lanes], left[:, lanes:]
        gd, db = right[:, :lanes], right[:, lanes:]
        amp[0] = chan + (db - gd)
        amp[1] = gs + gd
        amp[2] = -chan - gs
        amp[3] = -db

    def spread(amp, i, q):
        names = [names_of(first, k, i * inner + q) for k in range(4)]
        for team in range(0, BATCH, TEAM):
            for k in range(4):
                at = q * BATCH + team
                add_rows(
                    accs[k],
                    names[k][team : team + TEAM],
                    [amp[k, at + u : at + u + 1, :] for u in range(TEAM)],
                )

    def repeat(amp, i):
        def batch(n, carry):
            q = flags[steps + i * inner + n]
            b = i * inner + q
            for u in range(BATCH):
                for k in range(4):
                    at = (k * BATCH + u) * batches + b
                    spot = pl.ds(jnp.where(first[at] == spare, idx[at], spare), 1)
                    accs[k][spot, :] = accs[k][spot, :] + amp[k, pl.ds(q * BATCH + u, 1), :]
            return carry

        lax.fori_loop(0, flags[i], batch, 0)

    def stage(i, w, *, ahead=None, now=True, before=True, late=None):
        for q in range(inner):
            if before and q == inner // 2:
                analyse(duos[1 - w], amps[1 - w])
            if ahead is not None:
                collect(volts[1 - w], ahead, q)
            if now:
                model(volts[w], duos[w], i, q)
            if late is not None:
                spread(amps[w], late, q)
        if late is not None:
            repeat(amps[w], late)

    for q in range(inner):
        collect(volts0, 0, q)
    stage(0, 0, ahead=1, before=False)
    stage(1, 1, ahead=2)

    def pair(j, carry):
        for w in range(2):
            i = 2 * j + w
            stage(i, w, ahead=jnp.minimum(i + 1, steps - 1), late=i - 2)
        return carry

    lax.fori_loop(1, steps // 2, pair, 0)
    stage(steps, 0, now=False, late=steps - 2)
    stage(steps + 1, 1, now=False, before=False, late=steps - 1)
    low = lax.broadcasted_iota(jnp.int32, (half, lanes), 1) < half

    def pack(c, carry):
        for s in range(per_out):
            peer = c * per_out + s
            at = pl.multiple_of(peer * 2 * half, 2 * half)
            upper = pl.ds(at + half, half)
            at = pl.ds(at, half)
            one = sum(acc[at, :] for acc in accs)
            two = sum(acc[upper, :] for acc in accs)
            xbuf[peer, 0] = jnp.where(low, one, pltpu.roll(two, half, 1))
            xbuf[peer, 1] = jnp.where(low, pltpu.roll(one, half, 1), two)
        ship(c).start()
        return carry

    lax.fori_loop(0, n_out, pack, 0)
    for c in range(n_out):
        ship(c).wait()


def residual_kernel(
    rows, slots, idx_hbm, first_hbm, flags_hbm, cond_hbm, x_hbm, v_hbm, out_hbm,
    idx, first, flags, cond, xbuf, vbuf, low0, high0, low1, high1, own_sem, in_sem, v_sem, out_sem,
):
    nodes = vbuf.shape[1]
    half = slots // 2
    n_in = in_sem.shape[0]
    n_out = out_sem.shape[0]
    width = nodes // n_out
    peers = xbuf.shape[0] // half
    per_in = peers // n_in

    def fetch(c):
        part = pl.ds(c * per_in * half, per_in * half)
        return pltpu.make_async_copy(x_hbm.at[part], xbuf.at[part], in_sem.at[c])

    def ship(c):
        cols = pl.ds(c * width, width)
        return pltpu.make_async_copy(vbuf.at[:, cols], out_hbm.at[:, cols], out_sem.at[c])

    v_copy = pltpu.make_async_copy(v_hbm, vbuf, v_sem)
    own = [
        pltpu.make_async_copy(source, copy, own_sem.at[i])
        for i, (source, copy) in enumerate([(first_hbm, first), (flags_hbm, flags), (idx_hbm, idx), (cond_hbm, cond)])
    ]
    own[0].start()
    fetch(0).start()
    for copy in own[1:]:
        copy.start()
    for c in range(1, n_in):
        fetch(c).start()
    v_copy.start()

    def clear(i, carry):
        for acc in (low0, high0, low1, high1):
            acc[pl.ds(pl.multiple_of(i * 256, 256), 256), :] = jnp.zeros((256, 128), F32)
        return carry

    lax.fori_loop(0, nodes // 256, clear, 0)

    tables = ((low0, high0), (low1, high1))
    for copy in own:
        copy.wait()

    def tail(ref, offset):
        return ref.at[pl.ds(offset, ref.shape[0] - offset)]

    def group(c, carry):
        fetch(c).wait()

        def slot_group(i, carry):
            for w in range(16):
                j = i * 16 + w
                name, row = c * (per_in * slots) + j, c * (per_in * half) + j
                for team in range(0, BATCH, TEAM):
                    for h in range(2):
                        add_rows(
                            tables[(team // TEAM) % 2][h],
                            [tail(first, q * slots + h * half)[name] for q in range(team, team + TEAM)],
                            [tail(xbuf, q * half)[pl.ds(row, 1), :] for q in range(team, team + TEAM)],
                        )
            return carry

        lax.fori_loop(0, half // 16, slot_group, 0)

        def repeat(n, carry):
            i = flags[n_in + c * half + n]
            for q in range(BATCH):
                p = c * per_in + q
                x = xbuf[pl.ds(p * half + i, 1), :]
                for h in range(2):
                    at = p * slots + h * half + i
                    spot = pl.ds(jnp.where(first[at] == nodes, idx[at], nodes), 1)
                    table = tables[q % 2][h]
                    table[spot, :] = table[spot, :] + x
            return carry

        lax.fori_loop(0, flags[c], repeat, 0)
        return carry

    lax.fori_loop(0, n_in, group, 0)
    v_copy.wait()
    low = lax.broadcasted_iota(jnp.int32, (128, 128), 1) < rows

    def finish(c, carry):
        def turn(b, carry):
            for w in range(8):
                at = pl.multiple_of(c * width + (b * 8 + w) * 256, 256)
                one, two = pl.ds(at, 128), pl.ds(at + 128, 128)
                both = jnp.where(low, low0[one, :] + low1[one, :], high0[two, :] + high1[two, :])
                both = both + pltpu.roll(jnp.where(low, low0[two, :] + low1[two, :], high0[one, :] + high1[one, :]), rows, 1)
                both = both.T
                vbuf[:, one] = vbuf[:, one] * cond[:, one] + both[:rows]
                vbuf[:, two] = vbuf[:, two] * cond[:, two] + both[rows:]
            return carry

        lax.fori_loop(0, width // 2048, turn, 0)
        ship(c).start()
        return carry

    lax.fori_loop(0, n_out, finish, 0)
    for c in range(n_out):
        ship(c).wait()


def split_repeats(names, axis, spare):
    columns = [lax.index_in_dim(names, i, axis, keepdims=False) for i in range(names.shape[axis])]
    seen = [jnp.zeros(columns[0].shape, jnp.bool_)]
    for i in range(1, len(columns)):
        hit = columns[i] == columns[0]
        for j in range(1, i):
            hit = hit | (columns[i] == columns[j])
        seen.append(hit)
    seen = jnp.stack(seen, axis) & (names != spare)
    return jnp.where(seen, spare, names), seen


def marked(flags):
    n = flags.shape[1]
    place = jnp.arange(n, dtype=jnp.int32)
    rank = jnp.sum((flags[:, None, :] & (place[None, None, :] < place[None, :, None])).astype(jnp.int32), axis=2)
    hit = flags[:, None, :] & (rank[:, None, :] == place[None, :, None])
    order = jnp.sum(jnp.where(hit, place[None, None, :], 0), axis=2)
    return jnp.concatenate([jnp.sum(flags.astype(jnp.int32), axis=1), order.reshape(-1)])


ANY = pl.BlockSpec(memory_space=pl.ANY)
ROOM = pltpu.CompilerParams(vmem_limit_bytes=60 * 2**20)


def per_device(voltage, node_cond, model_table, model_index, send_nodes, term_slot):
    rows, nodes = voltage.shape
    senders = send_nodes.shape[1]
    groups = send_nodes.shape[2]
    slots = send_nodes.shape[3]
    half = slots // 2
    peers = senders * groups
    lanes = rows * groups
    tr_local = term_slot.shape[1] // groups
    send_list = send_nodes.reshape(-1)

    outgoing = pl.pallas_call(
        lambda *refs: pick_kernel(rows, slots, *refs),
        out_shape=jax.ShapeDtypeStruct((peers * half, lanes), F32),
        in_specs=[ANY, ANY],
        out_specs=ANY,
        scratch_shapes=[
            pltpu.SMEM((peers * slots,), jnp.int32),
            pltpu.VMEM((rows, nodes), F32),
            pltpu.VMEM((nodes + 8, lanes), F32),
            pltpu.VMEM((peers * half, lanes), F32),
            pltpu.SemaphoreType.DMA,
            pltpu.SemaphoreType.DMA((8,)),
            pltpu.SemaphoreType.DMA((8,)),
        ],
        compiler_params=ROOM,
        name="pick",
    )(send_list, voltage)

    arrived = lax.all_to_all(outgoing.reshape(peers, half, lanes), ("node", "freq"), 0, 0, tiled=True)

    start = lax.axis_index("freq") * tr_local
    index = lax.dynamic_slice_in_dim(model_index, start, tr_local)
    slot_grid = lax.dynamic_slice_in_dim(term_slot, start, tr_local, axis=1)
    batches = tr_local // BATCH
    index = index.reshape(BATCH, batches).T.reshape(-1)
    slot_list = slot_grid.reshape(-1)
    slot_grid = slot_grid.reshape(4 * BATCH // TEAM, TEAM, batches)
    tr_first, tr_seen = split_repeats(slot_grid, 1, senders * slots)
    tr_first = tr_first.reshape(-1)
    tr_flags = marked(jnp.any(tr_seen, axis=(0, 1)).reshape(-1, STEP // BATCH))
    send_grid = send_list.reshape(peers // TEAM, TEAM, slots)
    send_first, send_seen = split_repeats(send_grid, 1, nodes)
    send_first = send_first.reshape(-1)
    send_flags = jnp.any(send_seen.reshape(peers // BATCH, BATCH, 2, half), axis=(1, 2))
    send_flags = marked(send_flags)
    cards = jnp.concatenate([model_table[:2], 1.0 / (1.0 + model_table[2:3]), model_table[3:]], axis=0)
    onehot = (index[:, None] == jnp.arange(cards.shape[1], dtype=jnp.int32)[None, :]).astype(F32)
    params = jnp.dot(onehot, cards.T, precision=HIGH)

    synthesis, analysis, slope_table = dft_tables(lanes)
    syn = np.zeros((2, 2, rows, 2, lanes))
    for f in range(2):
        for q in range(2):
            syn[f, q, :, q, :] = synthesis.T[f * rows : (f + 1) * rows]
    none = np.zeros((lanes, lanes))
    ana = np.concatenate(
        [np.block([[analysis.T, none], [none, slope_table.T]]), np.block([[slope_table.T, none], [none, slope_table.T]])],
        axis=1,
    )
    syn = split_weights(syn.reshape(2 * lanes, 2 * lanes))
    ana = split_weights(ana)

    returned = pl.pallas_call(
        device_kernel,
        out_shape=jax.ShapeDtypeStruct((senders, 2, half, lanes), F32),
        in_specs=[ANY] * 7,
        out_specs=ANY,
        scratch_shapes=[pltpu.SMEM(a.shape, a.dtype) for a in (slot_list, tr_first, tr_flags)]
        + [pltpu.VMEM(a.shape, a.dtype) for a in (params, syn, ana)]
        + [
            pltpu.VMEM((senders, 2, half, lanes), F32),
            pltpu.VMEM((senders * slots, lanes), F32),
        ]
        + [pltpu.VMEM((4, STEP, lanes), F32)] * 2
        + [pltpu.VMEM((STEP, 4 * lanes), F32)] * 2
        + [pltpu.VMEM((4, STEP, lanes), F32)] * 2
        + [pltpu.VMEM((senders * slots + 8, lanes), F32)] * 4
        + [pltpu.SemaphoreType.DMA((8,))] * 3,
        compiler_params=ROOM,
        name="devices",
    )(slot_list, tr_first, tr_flags, params, syn, ana, arrived.reshape(senders, 2, half, lanes))

    incoming = lax.all_to_all(returned.reshape(peers, half, lanes), ("node", "freq"), 0, 0, tiled=True)

    return pl.pallas_call(
        lambda *refs: residual_kernel(rows, slots, *refs),
        out_shape=jax.ShapeDtypeStruct((rows, nodes), F32),
        in_specs=[ANY] * 6,
        out_specs=ANY,
        scratch_shapes=[pltpu.SMEM(a.shape, a.dtype) for a in (send_list, send_first, send_flags)]
        + [pltpu.VMEM((1, nodes), F32), pltpu.VMEM((peers * half, lanes), F32), pltpu.VMEM((rows, nodes), F32)]
        + [pltpu.VMEM((nodes + 8, lanes), F32)] * 4
        + [
            pltpu.SemaphoreType.DMA((4,)),
            pltpu.SemaphoreType.DMA((8,)),
            pltpu.SemaphoreType.DMA,
            pltpu.SemaphoreType.DMA((8,)),
        ],
        compiler_params=ROOM,
        name="residual",
    )(send_list, send_first, send_flags, node_cond.reshape(1, nodes), incoming.reshape(peers * half, lanes), voltage)


def solution(mesh):
    return jax.shard_map(
        per_device,
        mesh=mesh,
        in_specs=(
            P("freq", "node"),
            P("node"),
            P(),
            P("node"),
            P("node", None, None, None),
            P(None, "node"),
        ),
        out_specs=P("freq", "node"),
        check_vma=False,
    )
```
